256 devices in a mesh: row: 8 (over z_hi, y), col: 4 (over x), band: 8 (over z_lo, core).
Axes of the slice: x: 4, y: 4, z: 8 (z_hi: 2, z_lo: 4; z = z_hi * 4 + z_lo), core: 2. Of those that a mesh axis runs over, the one named last changes fastest.
Arguments:
- vis: bfloat16 [64, 4, 2, 512, 512], P('band', None, None, 'row', 'col'), may hold values from -200 to 200
- flags: int32 [64, 4, 512], P('band'), may hold values 0 or 1
- positions: float32 [4, 3, 512], replicated, may hold values from -4 to 4
- lmn: float32 [3, 8], replicated, may hold values from -3 to 3
- flux: float32 [64, 8], P('band'), may hold values from 0.5 to 2
- gains: float32 [64, 4, 2, 8, 512], P('band', None, None, None, ('row', 'col')), may hold values from -6 to 6
- duals: float32 [64, 4, 2, 8, 512], P('band', None, None, None, ('row', 'col')), may hold values from -2 to 2
Outputs:
- gains_out: float32 [64, 4, 2, 8, 512], P('band', None, None, None, ('row', 'col'))
- duals_out: float32 [64, 4, 2, 8, 512], P('band', None, None, None, ('row', 'col'))
The draws below stay inside these ranges and needn't reach their ends.
All inputs are finite; a program needn't handle non-finite values. No bound on the sum of `flags` on one device may be relied on, other than what follows from the above.
Results may differ from the reference program's by a relative error of at most 0.0003.
Values sent between devices are 32-bit elements; how exact they have to be, the bound alone decides.
A program may use at most 128 MiB of HBM per device.

```python
import math
import jax
import jax.numpy as jnp
from jax import lax

S = 512
DIRS = 8
F = 64
TSTEP = 4
ITERS = 2


def draw_vis(key, part):
    shape = (F, TSTEP, 2, S, S)
    base = jnp.clip(jax.random.normal(jax.random.fold_in(key, 11), shape, jnp.float32), -6.0, 6.0)
    station = 1.0 + 2.0 * jnp.arange(S, dtype=jnp.float32) / (S - 1)
    channel = 1.0 + 2.0 * jnp.arange(F, dtype=jnp.float32) / (F - 1)
    return (base * station[:, None] * channel[:, None, None, None, None]).astype(jnp.bfloat16)


def with_ends(values, rng, low, top_value):
    dims = values.shape
    place = [jax.random.randint(jax.random.fold_in(rng, axis), (), 0, dims[axis]) for axis in range(len(dims))]
    values = values.at[tuple(place)].set(low)
    longest = dims.index(max(dims))
    place[longest] = (place[longest] + 1) % dims[longest]
    return values.at[tuple(place)].set(top_value)


def shard_levels(key, extent, split, least, largest):
    level, own = 1.0, jax.random.fold_in(key, 6)
    for dim, blocks in split:
        heights = jnp.exp(jax.random.uniform(jax.random.fold_in(own, dim), (blocks,), jnp.float32, least / len(split), largest / len(split)))
        level = level * jnp.repeat(heights, extent[dim] // blocks).reshape([-1 if axis == dim else 1 for axis in range(len(extent))])
    return level


def bell_draw(own_key, dims, width, limit, shards=(), held_as=jnp.bfloat16):
    loudness = shard_levels(own_key, dims, shards, -0.22, 0.18) if shards else 1.0
    drawn = jax.random.normal(own_key, dims, jnp.float32) * width * loudness
    return jnp.minimum(jnp.maximum(drawn, -limit), limit).astype(held_as)


def setup_inputs(seed: int = 0) -> dict:
    arg_keys = jax.random.split(jax.random.key(seed), 8)
    vis = draw_vis(jax.random.fold_in(arg_keys[7], 71), 0)
    flags = with_ends((jax.random.randint(arg_keys[1], (F, TSTEP, S), 0, 8) < 7).astype(jnp.int32), jax.random.fold_in(arg_keys[1], 1), 0, 1)
    positions = bell_draw(arg_keys[2], (TSTEP, 3, S), 1.0, 4.0, (), jnp.float32)
    lmn = bell_draw(arg_keys[3], (3, DIRS), 0.5, 3.0, (), jnp.float32)
    flux = jnp.clip(jnp.exp(math.log(2.0) - 1.3862944 * jax.random.uniform(arg_keys[4], (F, DIRS), jnp.float32) ** shard_levels(arg_keys[4], (F, DIRS), ((0, 8),), -0.2, 0.2)), 0.5, 2.0)
    gains = bell_draw(arg_keys[5], (F, TSTEP, 2, DIRS, S), 1.0, 6.0, ((0, 8), (4, 32)), jnp.float32)
    duals = bell_draw(arg_keys[6], (F, TSTEP, 2, DIRS, S), 0.3, 2.0, ((0, 8), (4, 32)), jnp.float32)
    return dict(vis=vis, flags=flags, positions=positions, lmn=lmn, flux=flux, gains=gains, duals=duals)


PENALTY = 0.05
HIGH = lax.Precision.HIGHEST

def basis(count):
    grid = 2.0 * jnp.arange(count, dtype=jnp.float32) / (count - 1) - 1.0
    return jnp.stack([grid ** power for power in range(4)], axis=1)

def rotate(positions, lmn, freq):
    geometry = jnp.einsum('tks,kd->tds', positions, lmn, precision=HIGH)
    angle = 2.0 * math.pi * freq[:, None, None, None] * geometry[None]
    return (jnp.cos(angle), -jnp.sin(angle))

def complex_mul(a_re, a_im, b_re, b_im):
    return (a_re * b_re - a_im * b_im, a_re * b_im + a_im * b_re)

def solve_fit(rhs):
    full = basis(F)
    gram = jnp.dot(full.T, full, precision=HIGH)
    factor = jnp.linalg.cholesky(gram)
    flat = rhs.reshape(rhs.shape[0], -1)
    return jax.scipy.linalg.cho_solve((factor, True), flat).reshape(rhs.shape)

def reference(vis, flags, positions, lmn, flux, gains, duals):
    full = basis(F)
    freq = 1.0 + jnp.arange(F, dtype=jnp.float32) / F
    cos_all, sin_all = rotate(positions, lmn, freq)
    ids = jnp.arange(S, dtype=jnp.int32)
    distinct = (ids[:, None] != ids[None, :]).astype(jnp.float32)
    live = flags.astype(jnp.float32)

    def fit(gain, dual):
        rhs = jnp.einsum('fk,ftcds->ktcds', full, gain + dual, precision=HIGH)
        return solve_fit(rhs)

    def per_channel(items):
        visible, alive, row_re, row_im, col_re, col_im = items
        vis_re = visible[:, 0].astype(jnp.float32)
        vis_im = visible[:, 1].astype(jnp.float32)
        weight = alive[:, :, None] * alive[:, None, :] * distinct
        model_re = jnp.einsum('tdp,tdq->tpq', row_re, col_re, precision=HIGH) + jnp.einsum('tdp,tdq->tpq', row_im, col_im, precision=HIGH)
        model_im = jnp.einsum('tdp,tdq->tpq', row_im, col_re, precision=HIGH) - jnp.einsum('tdp,tdq->tpq', row_re, col_im, precision=HIGH)
        resid_re = weight * (vis_re - model_re)
        resid_im = weight * (vis_im - model_im)
        squares = jnp.sum(resid_re * resid_re + resid_im * resid_im)
        samples = jnp.sum(weight)
        sum_re = jnp.einsum('tpq,tdq->tdp', resid_re, col_re, precision=HIGH) - jnp.einsum('tpq,tdq->tdp', resid_im, col_im, precision=HIGH)
        sum_im = jnp.einsum('tpq,tdq->tdp', resid_re, col_im, precision=HIGH) + jnp.einsum('tpq,tdq->tdp', resid_im, col_re, precision=HIGH)
        denom = jnp.einsum('tpq,tdq->tdp', weight, col_re * col_re + col_im * col_im, precision=HIGH)
        return (jnp.stack([sum_re, sum_im, denom], axis=1), squares, samples)
    gain, dual = (gains, duals)
    coeffs = fit(gain, dual)
    for step in range(ITERS):
        target = jnp.einsum('fk,ktcds->ftcds', full, coeffs, precision=HIGH) - dual
        row_re, row_im = complex_mul(gain[:, :, 0], gain[:, :, 1], cos_all, sin_all)
        scale = flux[:, None, :, None]
        col_re = scale * row_re
        col_im = scale * row_im
        terms, squares, samples = lax.map(per_channel, (vis, live, row_re, row_im, col_re, col_im))
        rho = PENALTY * S * (jnp.sum(squares) / jnp.sum(samples) + 1e-06)
        num_re, num_im = complex_mul(cos_all, -sin_all, terms[:, :, 0], terms[:, :, 1])
        numer = jnp.stack([num_re, num_im], axis=2)
        denom = terms[:, :, 2:3]
        fresh = (numer + denom * gain + rho * target) / (denom + rho)
        gain = 0.5 * (gain + fresh)
        coeffs = fit(gain, dual)
        dual = dual + gain - jnp.einsum('fk,ktcds->ftcds', full, coeffs, precision=HIGH)
    return (gain, dual)
```

```python
import functools
import math

import jax
import jax.numpy as jnp
import numpy as np
from jax import lax
from jax.experimental import pallas as pl
from jax.experimental.pallas import tpu as pltpu
from jax.sharding import Mesh
from jax.sharding import PartitionSpec as P

S = 512
F = 64
ITERS = 2
PENALTY = 0.05
AXES = ("zh", "y", "x", "zl", "core")
BAND = ("zl", "core")
ROW = ("zh", "y")
OWN = ("zh", "y", "x")
MESH = pl.DeviceIdType.MESH
HIGH = lax.Precision.HIGHEST
F32 = jnp.float32
BF16 = jnp.bfloat16
PAIRS = 4
OWNED = 16
LANES = 128


def fit_polynomials():
    grid = 2.0 * np.arange(F, dtype=np.float64) / (F - 1) - 1.0
    powers = np.stack([grid**k for k in range(4)], axis=1)
    _, upper = np.linalg.qr(powers)
    return np.linalg.inv(upper)


def split(value):
    high = value.astype(BF16)
    return high, (value - high.astype(F32)).astype(BF16)


def kernel(
    vis_hbm, flags_ref, pos_ref, lmn_ref, flux_ref, gains_ref, duals_ref,
    gains_out, duals_out,
    vis_buf, wvis, weight, rmat, lhs, rhi,
    row_buf, col_buf, relay_buf, send_buf, num_buf, num_recv,
    t_buf, t_recv, fit_send, fit_recv, sq_send, sq_recv,
    flag_col, flag_row, geom_blk, flux_tab,
    vis_sem, row_s, row_r, rel_s, rel_r, own_s, fwd_s, col_r,
    num_s, num_r, t_s, t_r, sq_s, sq_r, fit_s, fit_r,
):
    me = {axis: lax.axis_index(axis) for axis in AXES}
    zh, y, x = me["zh"], me["y"], me["x"]

    def at(**moved):
        place = dict(me)
        place.update(moved)
        return tuple(place[axis] for axis in AXES)

    x_peers = [at(x=lax.rem(x + k, 4)) for k in range(1, 4)]
    plane_peers = [
        at(y=lax.rem(y + k // 4, 4), x=lax.rem(x + k % 4, 4)) for k in range(1, 16)
    ]
    line_peers = [
        at(
            zh=lax.rem(zh + k // 8, 2),
            zl=lax.rem(me["zl"] + (k // 2) % 4, 4),
            core=lax.rem(me["core"] + k % 2, 2),
        )
        for k in range(1, 16)
    ]
    band_peers = line_peers[:7]

    def push(src, dst, send_sem, recv_sem, device):
        return pltpu.make_async_remote_copy(
            src_ref=src, dst_ref=dst, send_sem=send_sem, recv_sem=recv_sem,
            device_id=device, device_id_type=MESH,
        )

    pending = []

    barrier = pltpu.get_barrier_semaphore()
    for peer in plane_peers + line_peers:
        pl.semaphore_signal(barrier, inc=1, device_id=peer, device_id_type=MESH)
    vis_copy = pltpu.make_async_copy(vis_hbm, vis_buf, vis_sem)
    vis_copy.start()

    lane = lax.broadcasted_iota(jnp.int32, (1, LANES), 1)
    half = lane // 64
    low = lane < 64
    is_im = (lane // 8) % 2 == 1
    sign = jnp.where(is_im, -1.0, 1.0).astype(F32)

    def swapped(value):
        return jnp.where(is_im, pltpu.roll(value, 8, 1), pltpu.roll(value, 120, 1))

    def both(value):
        return value + pltpu.roll(value, 64, 1)

    band = me["zl"] * 2 + me["core"]
    row = zh * 4 + y
    row_block = lax.div(row, 2)
    row_half = pl.multiple_of(lax.rem(row, 2) * 64, 64)
    own_at = pl.multiple_of(lax.rem(row, 2) * 64 + x * OWNED, OWNED)

    dir_hot = (
        lax.broadcasted_iota(jnp.int32, (8, LANES), 0)
        == lax.broadcasted_iota(jnp.int32, (8, LANES), 1) % 8
    ).astype(F32)
    flux_all = jnp.dot(flux_ref[...], dir_hot, precision=HIGH, preferred_element_type=F32)
    for fp in range(PAIRS):
        flux_tab[pl.ds(fp, 1), :] = jnp.where(
            low, flux_all[2 * fp : 2 * fp + 1], flux_all[2 * fp + 1 : 2 * fp + 2]
        )
    lmn_lanes = jnp.dot(lmn_ref[...], dir_hot, precision=HIGH, preferred_element_type=F32)
    time_of = (lane // 16) % 4
    block = pl.ds(pl.multiple_of(row_block * LANES, LANES), LANES)
    geom = jnp.zeros((LANES, LANES), F32)
    for t in range(4):
        here = jnp.concatenate([pos_ref[t, :, block], jnp.zeros((5, LANES), F32)], axis=0)
        pos_t = here.T
        axis_sum = (
            pos_t[:, 0:1] * lmn_lanes[0:1]
            + pos_t[:, 1:2] * lmn_lanes[1:2]
            + pos_t[:, 2:3] * lmn_lanes[2:3]
        )
        geom = jnp.where(time_of == t, axis_sum, geom)
    geom_blk[...] = geom
    geom = geom_blk[pl.ds(own_at, OWNED), :]

    cos, sin, gain, dual = [], [], [], []
    for fp in range(PAIRS):
        channel = (8 * band + 2 * fp + half).astype(F32)
        turns = (1.0 + channel / F) * geom
        angle = (2.0 * math.pi) * (turns - jnp.round(turns))
        cos.append(jnp.cos(angle))
        sin.append(sign * jnp.sin(angle))
        gain.append(gains_ref[2 * fp : 2 * fp + 2].reshape(LANES, OWNED).T)
        dual.append(duals_ref[2 * fp : 2 * fp + 2].reshape(LANES, OWNED).T)

    def turned(g):
        return [g[i] * cos[i] + swapped(g[i]) * sin[i] for i in range(PAIRS)]

    inv = fit_polynomials()
    quad = []
    for fp in range(PAIRS):
        channel = (8 * band + 2 * fp + half).astype(F32)
        grid = 2.0 * channel / (F - 1) - 1.0
        square = grid * grid
        quad.append([
            jnp.full((1, LANES), float(inv[0, 0]), F32),
            float(inv[1, 1]) * grid,
            float(inv[2, 2]) * square + float(inv[0, 2]),
            grid * (float(inv[3, 3]) * square + float(inv[1, 3])),
        ])

    def fit_start(stage, g, u):
        total = [g[i] + u[i] for i in range(PAIRS)]
        coef = [
            both(sum(quad[i][k] * total[i] for i in range(PAIRS))) for k in range(4)
        ]
        for j in range(2):
            fit_send[stage, j] = jnp.where(low, coef[2 * j], coef[2 * j + 1])
        for k, peer in enumerate(band_peers):
            copy = push(
                fit_send.at[stage], fit_recv.at[stage, k],
                fit_s.at[stage, k], fit_r.at[stage, k], peer,
            )
            copy.start()
            pending.append(copy)

    def fit_finish(stage):
        for k, peer in enumerate(band_peers):
            push(
                fit_send.at[stage], fit_recv.at[stage, k],
                fit_s.at[stage, k], fit_r.at[stage, k], peer,
            ).wait_recv()
        coef = []
        for j in range(2):
            value = fit_send[stage, j]
            for k in range(7):
                value = value + fit_recv[stage, k, j]
            turn = pltpu.roll(value, 64, 1)
            coef += [jnp.where(low, value, turn), jnp.where(low, turn, value)]
        return [sum(quad[i][k] * coef[k] for k in range(4)) for i in range(PAIRS)]

    own_col = 2 * zh + lax.div(y, 2)
    far_col = 2 * (1 - zh) + lax.div(y, 2)
    slot_rows = pl.ds(pl.multiple_of((lax.rem(y, 2) * 4 + x) * OWNED, OWNED), OWNED)
    x_rows = pl.ds(pl.multiple_of(x * OWNED, OWNED), OWNED)
    near = lax.div(x, 2) == zh

    def gather_start(it):
        src = send_buf.at[it]
        copies = [push(src, relay_buf.at[it], rel_s.at[it], rel_r.at[it], at(zh=1 - zh))]
        for k in range(1, 4):
            copies.append(push(
                src, col_buf.at[it, :, slot_rows], own_s.at[it, k],
                col_r.at[it, lax.rem(y, 2) * 4 + x],
                at(y=lax.rem(y + k, 4), x=own_col),
            ))
        for k, peer in enumerate(x_peers):
            copies.append(push(
                src, row_buf.at[it, :, x_rows], row_s.at[it, k], row_r.at[it, k], peer,
            ))
        for copy in copies:
            copy.start()
        pending.extend(copies)
        row_buf[it, :, x_rows, :] = send_buf[it]

    def gather_relay(it):
        push(
            send_buf.at[it], relay_buf.at[it], rel_s.at[it], rel_r.at[it], at(zh=1 - zh)
        ).wait_recv()
        src = relay_buf.at[it]
        for k in range(1, 4):
            copy = push(
                src, col_buf.at[it, :, slot_rows], fwd_s.at[it, k],
                col_r.at[it, lax.rem(y, 2) * 4 + x],
                at(y=lax.rem(y + k, 4), x=far_col),
            )
            copy.start()
            pending.append(copy)

        same_row = push(
            src, col_buf.at[it, :, slot_rows], fwd_s.at[it, 0],
            col_r.at[it, lax.rem(y, 2) * 4 + x], at(x=far_col),
        )

        @pl.when(x != far_col)
        def _():
            same_row.start()

        @pl.when(x == far_col)
        def _():
            col_buf[it, :, slot_rows, :] = relay_buf[it]

    def gather_finish(it):
        for k, peer in enumerate(x_peers):
            push(
                send_buf.at[it], row_buf.at[it, :, x_rows], row_s.at[it, k],
                row_r.at[it, k], peer,
            ).wait_recv()
        for j in range(8):
            from_y = lax.rem(x, 2) * 2 + j // 4
            copy = push(
                send_buf.at[it], col_buf.at[it, :, OWNED * j : OWNED * (j + 1)],
                own_s.at[it, 0], col_r.at[it, j], at(x=lax.rem(x + 1, 4)),
            )
            arrives = jnp.logical_or(
                from_y != y, jnp.logical_and(jnp.logical_not(near), x != j % 4)
            )

            @pl.when(arrives)
            def _(copy=copy):
                copy.wait_recv()

            @pl.when(jnp.logical_and(from_y == y, near))
            def _(j=j):
                col_buf[it, :, OWNED * j : OWNED * (j + 1), :] = row_buf[
                    it, :, OWNED * (j % 4) : OWNED * (j % 4 + 1), :
                ]

    for fp in range(PAIRS):
        send_buf[0, fp] = gain[fp] * cos[fp] + swapped(gain[fp]) * sin[fp]

    pl.semaphore_wait(barrier, 30)
    gather_start(0)
    fit_start(0, gain, dual)

    pair_hot = (
        lax.broadcasted_iota(jnp.int32, (8, LANES), 0)
        == lax.broadcasted_iota(jnp.int32, (8, LANES), 1) // 16
    ).astype(F32)
    col_block = pl.ds(pl.multiple_of(x * LANES, LANES), LANES)
    samples = jnp.zeros((4, 1), F32)
    for fp in range(PAIRS):
        for place, table in ((col_block, flag_col), (block, flag_row)):
            live = jnp.concatenate(
                [flags_ref[2 * fp, :, place], flags_ref[2 * fp + 1, :, place]], axis=0
            ).astype(F32)
            table[fp] = lax.dot_general(
                live, pair_hot, (((0,), (0,)), ((), ())), preferred_element_type=F32
            )
        for f in (2 * fp, 2 * fp + 1):
            count = jnp.sum(flags_ref[f].astype(F32), axis=1, keepdims=True)
            samples = samples + count * (count - 1.0)
    samples = jnp.sum(samples, axis=0, keepdims=True)

    rmat[...] = jnp.zeros_like(rmat)
    gather_relay(0)

    vis_copy.wait()
    row_id = row * 64 + lax.broadcasted_iota(jnp.int32, (64, LANES), 0)
    col_id = x * LANES + lax.broadcasted_iota(jnp.int32, (64, LANES), 1)
    distinct = (row_id != col_id).astype(F32)

    def prepare(fp, carry):
        row_flags = flag_row[fp, pl.ds(row_half, 64), :]
        for f2 in range(2):
            f = 2 * fp + f2
            for t in range(4):
                at_lane = 64 * f2 + 16 * t
                w = row_flags[:, at_lane : at_lane + 1] * distinct
                w = w * flags_ref[f, t : t + 1, col_block].astype(F32)
                weight[f, t] = w
                wvis[f, t, :, 0:LANES] = w * vis_buf[f, t, 0].astype(F32)
                wvis[f, t, :, LANES:] = w * vis_buf[f, t, 1].astype(F32)
        return carry

    lax.fori_loop(0, PAIRS, prepare, 0)

    def products(it):
        def arrange(fp, carry):
            flux = flux_tab[pl.ds(fp, 1), :]
            b = col_buf[it, fp] * flux
            t_buf[it, pl.ds(fp, 1), :] = jnp.sum(b * b * flag_col[fp], axis=0, keepdims=True)
            turned_b = b.T
            p = row_buf[it, fp]
            p_high = p.astype(BF16).astype(F32)
            p_low = p - p_high
            for f2 in range(2):
                f = 2 * fp + f2
                for part, value in ((0, p_high), (64, p_low)):
                    other = pltpu.roll(value, 64, 1)
                    pieces = (value, other) if f2 == 0 else (other, value)
                    lhs[f, part : part + 64, :] = jnp.where(low, *pieces).astype(BF16)
                for t in range(4):
                    start = 64 * f2 + 16 * t
                    left = turned_b[start : start + 16]
                    right = jnp.concatenate([-left[8:16], left[0:8]], axis=0)
                    high, rest = split(jnp.concatenate([left, right], axis=1))
                    rmat[f, t, 16 * t : 16 * t + 16, :] = high
                    rmat[f, t, 64 + 16 * t : 64 + 16 * t + 16, :] = rest
            return carry

        lax.fori_loop(0, PAIRS, arrange, 0)

        def residual(f, squares):
            for t in range(4):
                model = jnp.dot(lhs[f], rmat[f, t], preferred_element_type=F32)
                model = model[0:64] + model[64:128]
                w = weight[f, t]
                r = wvis[f, t] - jnp.concatenate([w, w], axis=1) * model
                high, rest = split(r)
                rhi[f, t, 0:64, :] = high
                rhi[f, t, 64:128, :] = rest
                squares = squares + jnp.sum((r * r).reshape(8, 8, 2 * LANES), axis=0)
            return squares

        squares = lax.fori_loop(0, 8, residual, jnp.zeros((8, 2 * LANES), F32))
        squares = squares[:, 0:LANES] + squares[:, LANES:]
        return jnp.sum(squares, axis=0, keepdims=True)

    def numerators(it):
        def pair(fp, carry):
            halves = []
            for f2 in range(2):
                f = 2 * fp + f2
                total = jnp.zeros((LANES, LANES), F32)
                for t in range(4):
                    total = total + lax.dot_general(
                        rhi[f, t], rmat[f, t], (((1,), (1,)), ((), ())),
                        preferred_element_type=F32,
                    )
                halves.append(both(total[0:64] + total[64:128]))
            num_buf[it, fp] = jnp.where(low, halves[0], halves[1])
            return carry

        lax.fori_loop(0, PAIRS, pair, 0)

    def squares_start(it, stage, value, peers):
        sq_send[it, stage] = value
        for k, peer in enumerate(peers):
            copy = push(
                sq_send.at[it, stage], sq_recv.at[it, stage, k],
                sq_s.at[it, stage, k], sq_r.at[it, stage, k], peer,
            )
            copy.start()
            pending.append(copy)

    def squares_finish(it, stage, peers):
        total = sq_send[it, stage]
        for k, peer in enumerate(peers):
            push(
                sq_send.at[it, stage], sq_recv.at[it, stage, k],
                sq_s.at[it, stage, k], sq_r.at[it, stage, k], peer,
            ).wait_recv()
        for k in range(15):
            total = total + sq_recv[it, stage, k]
        return total

    def exchange_start(it):
        for k, peer in enumerate(x_peers):
            there = lax.rem(x + k + 1, 4)
            rows = pl.ds(pl.multiple_of(there * OWNED, OWNED), OWNED)
            copy = push(
                num_buf.at[it, :, rows], num_recv.at[it, k],
                num_s.at[it, k], num_r.at[it, k], peer,
            )
            copy.start()
            pending.append(copy)

    def exchange_finish(it):
        for k, peer in enumerate(x_peers):
            push(
                num_buf.at[it, :, x_rows], num_recv.at[it, k],
                num_s.at[it, k], num_r.at[it, k], peer,
            ).wait_recv()
            push(t_buf.at[it], t_recv.at[it, k], t_s.at[it, k], t_r.at[it, k], peer).wait_recv()
        num = num_buf[it, :, x_rows, :]
        power = t_buf[it]
        for k in range(3):
            num = num + num_recv[it, k]
            power = power + t_recv[it, k]
        power = power + swapped(power)
        return num, power

    for it in range(ITERS):
        if it > 0:
            gather_relay(it)
        gather_finish(it)
        squares = products(it)
        squares_start(it, 0, squares, plane_peers)
        for k, peer in enumerate(x_peers):
            copy = push(t_buf.at[it], t_recv.at[it, k], t_s.at[it, k], t_r.at[it, k], peer)
            copy.start()
            pending.append(copy)
        numerators(it)
        exchange_start(it)
        squares = squares_finish(it, 0, plane_peers)
        squares = jnp.sum(squares, axis=1, keepdims=True)
        squares_start(it, 1, jnp.where(lane == 0, squares, jnp.where(lane == 1, samples, 0.0)), line_peers)
        smooth = fit_finish(it)
        if it > 0:
            dual = [dual[i] + gain[i] - smooth[i] for i in range(PAIRS)]
        num, power = exchange_finish(it)
        parts = []
        for i in range(PAIRS):
            target = smooth[i] - dual[i]
            mine = send_buf[it, i] * flux_tab[i : i + 1, :]
            mine = mine * mine
            live = flag_row[i, pl.ds(own_at, OWNED), :]
            den = live * (power[i : i + 1] - live * (mine + swapped(mine)))
            numer = num[i] * cos[i] - swapped(num[i]) * sin[i]
            parts.append((numer + den * gain[i], den, target))
        total = squares_finish(it, 1, line_peers)
        count = 0.5 * jnp.sum(jnp.where(lane == 1, total, 0.0), axis=1, keepdims=True)
        total = jnp.sum(jnp.where(lane == 0, total, 0.0), axis=1, keepdims=True)
        rho = PENALTY * S * (total / count + 1e-06)
        gain = [
            0.5 * (gain[i] + (top + rho * target) / (den + rho))
            for i, (top, den, target) in enumerate(parts)
        ]
        if it + 1 < ITERS:
            for i, value in enumerate(turned(gain)):
                send_buf[it + 1, i] = value
            gather_start(it + 1)
        fit_start(it + 1, gain, dual)

    for i in range(PAIRS):
        gains_out[2 * i : 2 * i + 2] = gain[i].T.reshape(2, 4, 2, 8, OWNED)
    smooth = fit_finish(ITERS)
    for i in range(PAIRS):
        value = dual[i] + gain[i] - smooth[i]
        duals_out[2 * i : 2 * i + 2] = value.T.reshape(2, 4, 2, 8, OWNED)

    for copy in pending:
        copy.wait_send()
    for it in range(ITERS):
        same_row = push(
            relay_buf.at[it], col_buf.at[it, :, slot_rows], fwd_s.at[it, 0],
            col_r.at[it, 0], at(x=lax.rem(x + 1, 4)),
        )

        @pl.when(x != far_col)
        def _(same_row=same_row):
            same_row.wait_send()


def shards(vis, flags, positions, lmn, flux, gains, duals):
    vmem = pl.BlockSpec(memory_space=pltpu.VMEM)
    dma = pltpu.SemaphoreType.DMA
    return pl.pallas_call(
        kernel,
        name="admm",
        out_shape=(
            jax.ShapeDtypeStruct(gains.shape, F32),
            jax.ShapeDtypeStruct(duals.shape, F32),
        ),
        in_specs=[pl.BlockSpec(memory_space=pl.ANY)] + [vmem] * 6,
        out_specs=(vmem, vmem),
        scratch_shapes=[
            pltpu.VMEM((8, 4, 2, 64, LANES), BF16),
            pltpu.VMEM((8, 4, 64, 2 * LANES), F32),
            pltpu.VMEM((8, 4, 64, LANES), F32),
            pltpu.VMEM((8, 4, LANES, 2 * LANES), BF16),
            pltpu.VMEM((8, LANES, LANES), BF16),
            pltpu.VMEM((8, 4, LANES, 2 * LANES), BF16),
            pltpu.VMEM((ITERS, PAIRS, 64, LANES), F32),
            pltpu.VMEM((ITERS, PAIRS, LANES, LANES), F32),
            pltpu.VMEM((ITERS, PAIRS, OWNED, LANES), F32),
            pltpu.VMEM((ITERS, PAIRS, OWNED, LANES), F32),
            pltpu.VMEM((ITERS, PAIRS, 64, LANES), F32),
            pltpu.VMEM((ITERS, 3, PAIRS, OWNED, LANES), F32),
            pltpu.VMEM((ITERS, PAIRS, LANES), F32),
            pltpu.VMEM((ITERS, 3, PAIRS, LANES), F32),
            pltpu.VMEM((ITERS + 1, 2, OWNED, LANES), F32),
            pltpu.VMEM((ITERS + 1, 7, 2, OWNED, LANES), F32),
            pltpu.VMEM((ITERS, 2, 1, LANES), F32),
            pltpu.VMEM((ITERS, 2, 15, 1, LANES), F32),
            pltpu.VMEM((PAIRS, LANES, LANES), F32),
            pltpu.VMEM((PAIRS, LANES, LANES), F32),
            pltpu.VMEM((LANES, LANES), F32),
            pltpu.VMEM((PAIRS, LANES), F32),
            dma,
            dma((ITERS, 3)), dma((ITERS, 3)),
            dma((ITERS,)), dma((ITERS,)),
            dma((ITERS, 4)), dma((ITERS, 4)), dma((ITERS, 8)),
            dma((ITERS, 3)), dma((ITERS, 3)),
            dma((ITERS, 3)), dma((ITERS, 3)),
            dma((ITERS, 2, 15)), dma((ITERS, 2, 15)),
            dma((ITERS + 1, 7)), dma((ITERS + 1, 7)),
        ],
        compiler_params=pltpu.CompilerParams(
            collective_id=0, has_side_effects=True, vmem_limit_bytes=48 * 1024 * 1024
        ),
    )(vis, flags, positions, lmn, flux, gains, duals)


def solution(mesh):
    finer = Mesh(mesh.devices.reshape(2, 4, mesh.shape["col"], 4, 2), AXES)
    return jax.shard_map(
        shards,
        mesh=finer,
        in_specs=(
            P(BAND, None, None, ROW, "x"),
            P(BAND, None, None),
            P(),
            P(),
            P(BAND, None),
            P(BAND, None, None, None, OWN),
            P(BAND, None, None, None, OWN),
        ),
        out_specs=(P(BAND, None, None, None, OWN), P(BAND, None, None, None, OWN)),
        check_vma=False,
    )
```

```python
import functools
import math

import jax
import jax.numpy as jnp
import numpy as np
from jax import lax
from jax.experimental import pallas as pl
from jax.experimental.pallas import tpu as pltpu
from jax.sharding import Mesh
from jax.sharding import PartitionSpec as P

S = 512
F = 64
ITERS = 2
PENALTY = 0.05
AXES = ("zh", "y", "x", "zl", "core")
BAND = ("zl", "core")
ROW = ("zh", "y")
OWN = ("zh", "y", "x")
MESH = pl.DeviceIdType.MESH
HIGH = lax.Precision.HIGHEST
F32 = jnp.float32
BF16 = jnp.bfloat16
PAIRS = 4
CHUNKS = 2
GATHERS = 3
OWNED = 16
LANES = 128


def fit_polynomials():
    grid = 2.0 * np.arange(F, dtype=np.float64) / (F - 1) - 1.0
    powers = np.stack([grid**k for k in range(4)], axis=1)
    _, upper = np.linalg.qr(powers)
    return np.linalg.inv(upper)


def split(value):
    high = value.astype(BF16)
    return high, (value - high.astype(F32)).astype(BF16)


def kernel(
    vis_hbm, flags_hbm, pos_hbm, lmn_hbm, flux_hbm, gains_hbm, duals_hbm,
    gains_out, duals_out,
    vis_buf, flags_ref, pos_ref, lmn_ref, flux_ref, gains_ref, duals_ref, wvis, weight, rmat, lhs, rhi,
    row_buf, col_buf, relay_buf, send_buf, num_buf, num_recv,
    t_buf, t_recv, fit_send, fit_recv, sq_send, sq_recv,
    flag_col, flag_row, geom_blk, flux_tab,
    in_sem, row_s, row_r, rel_s, rel_r, own_s, fwd_s, col_r,
    num_s, num_r, t_s, t_r, sq_s, sq_r, fit_s, fit_r,
):
    me = {axis: lax.axis_index(axis) for axis in AXES}
    zh, y, x = me["zh"], me["y"], me["x"]

    def at(**moved):
        place = dict(me)
        place.update(moved)
        return tuple(place[axis] for axis in AXES)

    x_peers = [at(x=lax.rem(x + k, 4)) for k in range(1, 4)]
    plane_peers = [
        at(y=lax.rem(y + k // 4, 4), x=lax.rem(x + k % 4, 4)) for k in range(1, 16)
    ]
    line_peers = [
        at(
            zh=lax.rem(zh + k // 8, 2),
            zl=lax.rem(me["zl"] + (k // 2) % 4, 4),
            core=lax.rem(me["core"] + k % 2, 2),
        )
        for k in range(1, 16)
    ]
    band_peers = line_peers[:7]

    def push(src, dst, send_sem, recv_sem, device):
        return pltpu.make_async_remote_copy(
            src_ref=src, dst_ref=dst, send_sem=send_sem, recv_sem=recv_sem,
            device_id=device, device_id_type=MESH,
        )

    pending = []

    gains_copy, pos_copy, lmn_copy, flux_copy, duals_copy, flags_copy, vis_copy = (
        pltpu.make_async_copy(src, dst, in_sem.at[i])
        for i, (src, dst) in enumerate((
            (gains_hbm, gains_ref), (pos_hbm, pos_ref), (lmn_hbm, lmn_ref),
            (flux_hbm, flux_ref), (duals_hbm, duals_ref), (flags_hbm, flags_ref),
            (vis_hbm, vis_buf),
        ))
    )
    for copy in (gains_copy, pos_copy, lmn_copy, flux_copy, duals_copy, flags_copy, vis_copy):
        copy.start()

    barrier = pltpu.get_barrier_semaphore()
    for peer in plane_peers + line_peers:
        pl.semaphore_signal(barrier, inc=1, device_id=peer, device_id_type=MESH)

    lane = lax.broadcasted_iota(jnp.int32, (1, LANES), 1)
    half = lane // 64
    low = lane < 64
    is_im = (lane // 8) % 2 == 1
    sign = jnp.where(is_im, -1.0, 1.0).astype(F32)

    def swapped(value):
        return jnp.where(is_im, pltpu.roll(value, 8, 1), pltpu.roll(value, 120, 1))

    def both(value):
        return value + pltpu.roll(value, 64, 1)

    band = me["zl"] * 2 + me["core"]
    row = zh * 4 + y
    row_block = lax.div(row, 2)
    row_half = pl.multiple_of(lax.rem(row, 2) * 64, 64)
    own_at = pl.multiple_of(lax.rem(row, 2) * 64 + x * OWNED, OWNED)

    dir_hot = (
        lax.broadcasted_iota(jnp.int32, (8, LANES), 0)
        == lax.broadcasted_iota(jnp.int32, (8, LANES), 1) % 8
    ).astype(F32)
    time_of = (lane // 16) % 4
    block = pl.ds(pl.multiple_of(row_block * LANES, LANES), LANES)
    pos_copy.wait()
    lmn_copy.wait()
    lmn_lanes = jnp.dot(lmn_ref[...], dir_hot, precision=HIGH, preferred_element_type=F32)
    places = jnp.concatenate(
        [pos_ref[k, :, block] for k in range(3)] + [jnp.zeros((4, LANES), F32)], axis=0
    ).T
    geom = jnp.zeros((LANES, LANES), F32)
    for t in range(4):
        axis_sum = (
            places[:, t : t + 1] * lmn_lanes[0:1]
            + places[:, t + 4 : t + 5] * lmn_lanes[1:2]
            + places[:, t + 8 : t + 9] * lmn_lanes[2:3]
        )
        geom = jnp.where(time_of == t, axis_sum, geom)
    geom_blk[...] = geom
    geom = geom_blk[pl.ds(own_at, OWNED), :]

    def turned(g, i):
        return g * cos[i] + swapped(g) * sin[i]

    gains_copy.wait()
    cos, sin, gain, dual = [], [], [], []
    for fp in range(PAIRS):
        channel = (8 * band + 2 * fp + half).astype(F32)
        turns = (1.0 + channel / F) * geom
        angle = (2.0 * math.pi) * (turns - jnp.round(turns))
        cos.append(jnp.cos(angle))
        sin.append(sign * jnp.sin(angle))
        gain.append(gains_ref[2 * fp : 2 * fp + 2].reshape(LANES, OWNED).T)
        send_buf[0, fp] = turned(gain[fp], fp)
    duals_copy.wait()
    for fp in range(PAIRS):
        dual.append(duals_ref[2 * fp : 2 * fp + 2].reshape(LANES, OWNED).T)

    inv = fit_polynomials()
    quad = []
    for fp in range(PAIRS):
        channel = (8 * band + 2 * fp + half).astype(F32)
        grid = 2.0 * channel / (F - 1) - 1.0
        square = grid * grid
        quad.append([
            jnp.full((1, LANES), float(inv[0, 0]), F32),
            float(inv[1, 1]) * grid,
            float(inv[2, 2]) * square + float(inv[0, 2]),
            grid * (float(inv[3, 3]) * square + float(inv[1, 3])),
        ])

    def fit_start(stage, g, u):
        total = [g[i] + u[i] for i in range(PAIRS)]
        coef = [
            both(sum(quad[i][k] * total[i] for i in range(PAIRS))) for k in range(4)
        ]
        for j in range(2):
            fit_send[stage, j] = jnp.where(low, coef[2 * j], coef[2 * j + 1])
        for k, peer in enumerate(band_peers):
            copy = push(
                fit_send.at[stage], fit_recv.at[stage, k],
                fit_s.at[stage, k], fit_r.at[stage, k], peer,
            )
            copy.start()
            pending.append(copy)

    def fit_finish(stage):
        for k, peer in enumerate(band_peers):
            push(
                fit_send.at[stage], fit_recv.at[stage, k],
                fit_s.at[stage, k], fit_r.at[stage, k], peer,
            ).wait_recv()
        coef = []
        for j in range(2):
            value = fit_send[stage, j]
            for k in range(7):
                value = value + fit_recv[stage, k, j]
            turn = pltpu.roll(value, 64, 1)
            coef += [jnp.where(low, value, turn), jnp.where(low, turn, value)]
        return [sum(quad[i][k] * coef[k] for k in range(4)) for i in range(PAIRS)]

    own_col = 2 * zh + lax.div(y, 2)
    far_col = 2 * (1 - zh) + lax.div(y, 2)
    slot_rows = pl.ds(pl.multiple_of((lax.rem(y, 2) * 4 + x) * OWNED, OWNED), OWNED)
    x_rows = pl.ds(pl.multiple_of(x * OWNED, OWNED), OWNED)
    near = lax.div(x, 2) == zh

    own_slot = lax.rem(y, 2) * 4 + x

    def part(h):
        return pl.ds(h * (PAIRS // CHUNKS), PAIRS // CHUNKS)

    def across(slot, h):
        return push(
            send_buf.at[slot, part(h)], relay_buf.at[slot, part(h)],
            rel_s.at[slot, h], rel_r.at[slot, h], at(zh=1 - zh),
        )

    def gather_start(slot):
        copies = [across(slot, h) for h in range(CHUNKS)]
        for k, peer in enumerate(x_peers):
            copies.append(push(
                send_buf.at[slot], row_buf.at[slot, :, x_rows],
                row_s.at[slot, k], row_r.at[slot, k], peer,
            ))
        for h in range(CHUNKS):
            for k in range(1, 4):
                copies.append(push(
                    send_buf.at[slot, part(h)], col_buf.at[slot, part(h), slot_rows],
                    own_s.at[slot, k, h], col_r.at[slot, own_slot, h],
                    at(y=lax.rem(y + k, 4), x=own_col),
                ))
        for copy in copies:
            copy.start()
        pending.extend(copies)
        row_buf[slot, :, x_rows, :] = send_buf[slot]

    def to_far_col(slot, h):
        return push(
            relay_buf.at[slot, part(h)], col_buf.at[slot, part(h), slot_rows],
            fwd_s.at[slot, 0, h], col_r.at[slot, own_slot, h], at(x=far_col),
        )

    def gather_relay(slot):
        for h in range(CHUNKS):
            across(slot, h).wait_recv()
            for k in range(1, 4):
                copy = push(
                    relay_buf.at[slot, part(h)], col_buf.at[slot, part(h), slot_rows],
                    fwd_s.at[slot, k, h], col_r.at[slot, own_slot, h],
                    at(y=lax.rem(y + k, 4), x=far_col),
                )
                copy.start()
                pending.append(copy)

            @pl.when(x != far_col)
            def _(h=h):
                to_far_col(slot, h).start()

            @pl.when(x == far_col)
            def _(h=h):
                col_buf[slot, part(h), slot_rows, :] = relay_buf[slot, part(h)]

    def gather_finish(slot, h):
        if h == 0:
            for k, peer in enumerate(x_peers):
                push(
                    send_buf.at[slot], row_buf.at[slot, :, x_rows],
                    row_s.at[slot, k], row_r.at[slot, k], peer,
                ).wait_recv()
        for j in range(8):
            from_y = lax.rem(x, 2) * 2 + j // 4
            rows = slice(OWNED * j, OWNED * (j + 1))
            row_rows = slice(OWNED * (j % 4), OWNED * (j % 4 + 1))
            copy = push(
                send_buf.at[slot, part(h)], col_buf.at[slot, part(h), rows],
                own_s.at[slot, 0, h], col_r.at[slot, j, h], x_peers[0],
            )
            arrives = jnp.logical_or(
                from_y != y, jnp.logical_and(jnp.logical_not(near), x != j % 4)
            )

            @pl.when(arrives)
            def _(copy=copy):
                copy.wait_recv()

            @pl.when(jnp.logical_and(from_y == y, near))
            def _(rows=rows, row_rows=row_rows):
                col_buf[slot, part(h), rows, :] = row_buf[slot, part(h), row_rows, :]

    pl.semaphore_wait(barrier, 30)
    gather_start(0)
    fit_start(0, gain, dual)

    flux_copy.wait()
    flux_all = jnp.dot(flux_ref[...], dir_hot, precision=HIGH, preferred_element_type=F32)
    for fp in range(PAIRS):
        flux_tab[pl.ds(fp, 1), :] = jnp.where(
            low, flux_all[2 * fp : 2 * fp + 1], flux_all[2 * fp + 1 : 2 * fp + 2]
        )

    pair_hot = (
        lax.broadcasted_iota(jnp.int32, (8, LANES), 0)
        == lax.broadcasted_iota(jnp.int32, (8, LANES), 1) // 16
    ).astype(F32)
    col_block = pl.ds(pl.multiple_of(x * LANES, LANES), LANES)
    samples = jnp.zeros((4, 1), F32)
    flags_copy.wait()
    for fp in range(PAIRS):
        for place, table in ((col_block, flag_col), (block, flag_row)):
            live = jnp.concatenate(
                [flags_ref[2 * fp, :, place], flags_ref[2 * fp + 1, :, place]], axis=0
            ).astype(F32)
            table[fp] = lax.dot_general(
                live, pair_hot, (((0,), (0,)), ((), ())), preferred_element_type=F32
            )
        for f in (2 * fp, 2 * fp + 1):
            count = jnp.sum(flags_ref[f].astype(F32), axis=1, keepdims=True)
            samples = samples + count * (count - 1.0)
    samples = jnp.sum(samples, axis=0, keepdims=True)

    rmat[...] = jnp.zeros_like(rmat)
    gather_relay(0)
    smooth = fit_finish(0)
    for i in range(PAIRS):
        send_buf[1, i] = turned(smooth[i] - dual[i], i)
    gather_start(1)

    vis_copy.wait()
    row_id = row * 64 + lax.broadcasted_iota(jnp.int32, (64, LANES), 0)
    col_id = x * LANES + lax.broadcasted_iota(jnp.int32, (64, LANES), 1)
    distinct = (row_id != col_id).astype(F32)

    def prepare(fp, carry):
        row_flags = flag_row[fp, pl.ds(row_half, 64), :]
        for f2 in range(2):
            f = 2 * fp + f2
            for t in range(4):
                at_lane = 64 * f2 + 16 * t
                w = row_flags[:, at_lane : at_lane + 1] * distinct
                w = w * flags_ref[f, t : t + 1, col_block].astype(F32)
                weight[f, t] = w
                wvis[f, t, :, 0:LANES] = w * vis_buf[f, t, 0].astype(F32)
                wvis[f, t, :, LANES:] = w * vis_buf[f, t, 1].astype(F32)
        return carry

    lax.fori_loop(0, PAIRS, prepare, 0)

    def arrange(it, fp):
        flux = flux_tab[pl.ds(fp, 1), :]
        b = col_buf[0, fp]
        p = row_buf[0, fp]
        if it > 0:
            b = b + col_buf[1, fp] * col_buf[2, fp]
            p = p + row_buf[1, fp] * row_buf[2, fp]
        b = b * flux
        t_buf[it, pl.ds(fp, 1), :] = jnp.sum(b * b * flag_col[fp], axis=0, keepdims=True)
        turned_b = b.T
        p_high = p.astype(BF16).astype(F32)
        p_low = p - p_high
        for f2 in range(2):
            f = 2 * fp + f2
            for start, value in ((0, p_high), (64, p_low)):
                other = pltpu.roll(value, 64, 1)
                pieces = (value, other) if f2 == 0 else (other, value)
                lhs[f, start : start + 64, :] = jnp.where(low, *pieces).astype(BF16)
            for t in range(4):
                start = 64 * f2 + 16 * t
                left = turned_b[start : start + 16]
                right = jnp.concatenate([-left[8:16], left[0:8]], axis=0)
                high, rest = split(jnp.concatenate([left, right], axis=1))
                rmat[f, t, 16 * t : 16 * t + 16, :] = high
                rmat[f, t, 64 + 16 * t : 64 + 16 * t + 16, :] = rest

    def products(it):
        def residual(f, squares):
            for t in range(4):
                model = jnp.dot(lhs[f], rmat[f, t], preferred_element_type=F32)
                model = model[0:64] + model[64:128]
                w = weight[f, t]
                r = wvis[f, t] - jnp.concatenate([w, w], axis=1) * model
                high, rest = split(r)
                rhi[f, t, 0:64, :] = high
                rhi[f, t, 64:128, :] = rest
                squares = squares + jnp.sum((r * r).reshape(8, 8, 2 * LANES), axis=0)
            return squares

        squares = jnp.zeros((8, 2 * LANES), F32)
        for h in range(CHUNKS):
            gather_finish(2 * it, h)
            first, end = h * PAIRS // CHUNKS, (h + 1) * PAIRS // CHUNKS

            def arranged(fp, carry):
                arrange(it, fp)
                return carry

            lax.fori_loop(first, end, arranged, 0)
            squares = lax.fori_loop(2 * first, 2 * end, residual, squares)
        squares = squares[:, 0:LANES] + squares[:, LANES:]
        return jnp.sum(squares, axis=0, keepdims=True)

    def numerators(it):
        def pair(fp, carry):
            halves = []
            for f2 in range(2):
                f = 2 * fp + f2
                total = jnp.zeros((LANES, LANES), F32)
                for t in range(4):
                    total = total + lax.dot_general(
                        rhi[f, t], rmat[f, t], (((1,), (1,)), ((), ())),
                        preferred_element_type=F32,
                    )
                halves.append(both(total[0:64] + total[64:128]))
            num_buf[it, fp] = jnp.where(low, halves[0], halves[1])
            return carry

        lax.fori_loop(0, PAIRS, pair, 0)

    def squares_start(it, stage, value, peers):
        sq_send[it, stage] = value
        for k, peer in enumerate(peers):
            copy = push(
                sq_send.at[it, stage], sq_recv.at[it, stage, k],
                sq_s.at[it, stage, k], sq_r.at[it, stage, k], peer,
            )
            copy.start()
            pending.append(copy)

    def squares_finish(it, stage, peers):
        total = sq_send[it, stage]
        for k, peer in enumerate(peers):
            push(
                sq_send.at[it, stage], sq_recv.at[it, stage, k],
                sq_s.at[it, stage, k], sq_r.at[it, stage, k], peer,
            ).wait_recv()
        for k in range(15):
            total = total + sq_recv[it, stage, k]
        return total

    def exchange_start(it):
        for k, peer in enumerate(x_peers):
            there = lax.rem(x + k + 1, 4)
            rows = pl.ds(pl.multiple_of(there * OWNED, OWNED), OWNED)
            copy = push(
                num_buf.at[it, :, rows], num_recv.at[it, k],
                num_s.at[it, k], num_r.at[it, k], peer,
            )
            copy.start()
            pending.append(copy)

    def exchange_finish(it):
        for k, peer in enumerate(x_peers):
            push(
                num_buf.at[it, :, x_rows], num_recv.at[it, k],
                num_s.at[it, k], num_r.at[it, k], peer,
            ).wait_recv()
            push(t_buf.at[it], t_recv.at[it, k], t_s.at[it, k], t_r.at[it, k], peer).wait_recv()
        num = num_buf[it, :, x_rows, :]
        power = t_buf[it]
        for k in range(3):
            num = num + num_recv[it, k]
            power = power + t_recv[it, k]
        power = power + swapped(power)
        return num, power

    def solve_for(p, live, flux, power):
        b = p * flux
        b = b * b
        return live * (power - live * (b + swapped(b)))

    for it in range(ITERS):
        squares = products(it)
        squares_start(it, 0, squares, plane_peers)
        for k, peer in enumerate(x_peers):
            copy = push(t_buf.at[it], t_recv.at[it, k], t_s.at[it, k], t_r.at[it, k], peer)
            copy.start()
            pending.append(copy)
        numerators(it)
        exchange_start(it)
        if it == 0:
            gather_relay(1)
            num, power = exchange_finish(it)
            send_buf[2] = num
            gather_start(2)
        squares = squares_finish(it, 0, plane_peers)
        squares = jnp.sum(squares, axis=1, keepdims=True)
        squares_start(
            it, 1,
            jnp.where(lane == 0, squares, jnp.where(lane == 1, samples, 0.0)), line_peers,
        )
        if it == 0:
            gather_relay(2)
        else:
            smooth = fit_finish(it)
            dual = [dual[i] + gain[i] - smooth[i] for i in range(PAIRS)]
            num, power = exchange_finish(it)
        parts = []
        for i in range(PAIRS):
            target = smooth[i] - dual[i]
            live = flag_row[i, pl.ds(own_at, OWNED), :]
            den = solve_for(
                turned(gain[i], i), live, flux_tab[i : i + 1, :], power[i : i + 1]
            )
            numer = num[i] * cos[i] - swapped(num[i]) * sin[i]
            parts.append((numer + den * gain[i], den, target))
        total = squares_finish(it, 1, line_peers)
        count = 0.5 * jnp.sum(jnp.where(lane == 1, total, 0.0), axis=1, keepdims=True)
        total = jnp.sum(jnp.where(lane == 0, total, 0.0), axis=1, keepdims=True)
        rho = PENALTY * S * (total / count + 1e-06)
        gain = [
            0.5 * (gain[i] + (top + rho * target) / (den + rho))
            for i, (top, den, target) in enumerate(parts)
        ]
        fit_start(it + 1, gain, dual)
        if it + 1 < ITERS:
            for h in range(CHUNKS):
                gather_finish(1, h)
            for i in range(PAIRS):
                flux, every = flux_tab[i : i + 1, :], power[i : i + 1]
                for buf, live in (
                    (row_buf, flag_row[i, pl.ds(row_half, 64), :]),
                    (col_buf, flag_col[i]),
                ):
                    p = buf[0, i]
                    den = solve_for(p, live, flux, every)
                    share = 0.5 / (den + rho)
                    buf[0, i] = 0.5 * p + share * (den * p + rho * buf[1, i])
                    buf[1, i] = share

    for i in range(PAIRS):
        gains_out[2 * i : 2 * i + 2] = gain[i].T.reshape(2, 4, 2, 8, OWNED)
    smooth = fit_finish(ITERS)
    for i in range(PAIRS):
        value = dual[i] + gain[i] - smooth[i]
        duals_out[2 * i : 2 * i + 2] = value.T.reshape(2, 4, 2, 8, OWNED)

    for copy in pending:
        copy.wait_send()

    @pl.when(x != far_col)
    def _():
        for slot in range(GATHERS):
            for h in range(CHUNKS):
                to_far_col(slot, h).wait_send()


def shards(vis, flags, positions, lmn, flux, gains, duals):
    vmem = pl.BlockSpec(memory_space=pltpu.VMEM)
    positions = jnp.swapaxes(positions, 0, 1)
    dma = pltpu.SemaphoreType.DMA
    return pl.pallas_call(
        kernel,
        name="admm",
        out_shape=(
            jax.ShapeDtypeStruct(gains.shape, F32),
            jax.ShapeDtypeStruct(duals.shape, F32),
        ),
        in_specs=[pl.BlockSpec(memory_space=pltpu.HBM)] * 7,
        out_specs=(vmem, vmem),
        scratch_shapes=[
            pltpu.VMEM(vis.shape, BF16),
            pltpu.VMEM(flags.shape, jnp.int32),
            pltpu.VMEM(positions.shape, F32),
            pltpu.VMEM(lmn.shape, F32),
            pltpu.VMEM(flux.shape, F32),
            pltpu.VMEM(gains.shape, F32),
            pltpu.VMEM(duals.shape, F32),
            pltpu.VMEM((8, 4, 64, 2 * LANES), F32),
            pltpu.VMEM((8, 4, 64, LANES), F32),
            pltpu.VMEM((8, 4, LANES, 2 * LANES), BF16),
            pltpu.VMEM((8, LANES, LANES), BF16),
            pltpu.VMEM((8, 4, LANES, 2 * LANES), BF16),
            pltpu.VMEM((GATHERS, PAIRS, 64, LANES), F32),
            pltpu.VMEM((GATHERS, PAIRS, LANES, LANES), F32),
            pltpu.VMEM((GATHERS, PAIRS, OWNED, LANES), F32),
            pltpu.VMEM((GATHERS, PAIRS, OWNED, LANES), F32),
            pltpu.VMEM((ITERS, PAIRS, 64, LANES), F32),
            pltpu.VMEM((ITERS, 3, PAIRS, OWNED, LANES), F32),
            pltpu.VMEM((ITERS, PAIRS, LANES), F32),
            pltpu.VMEM((ITERS, 3, PAIRS, LANES), F32),
            pltpu.VMEM((ITERS + 1, 2, OWNED, LANES), F32),
            pltpu.VMEM((ITERS + 1, 7, 2, OWNED, LANES), F32),
            pltpu.VMEM((ITERS, 2, 1, LANES), F32),
            pltpu.VMEM((ITERS, 2, 15, 1, LANES), F32),
            pltpu.VMEM((PAIRS, LANES, LANES), F32),
            pltpu.VMEM((PAIRS, LANES, LANES), F32),
            pltpu.VMEM((LANES, LANES), F32),
            pltpu.VMEM((PAIRS, LANES), F32),
            dma((7,)),
            dma((GATHERS, 3)), dma((GATHERS, 3)),
            dma((GATHERS, CHUNKS)), dma((GATHERS, CHUNKS)),
            dma((GATHERS, 4, CHUNKS)), dma((GATHERS, 4, CHUNKS)),
            dma((GATHERS, 8, CHUNKS)),
            dma((ITERS, 3)), dma((ITERS, 3)),
            dma((ITERS, 3)), dma((ITERS, 3)),
            dma((ITERS, 2, 15)), dma((ITERS, 2, 15)),
            dma((ITERS + 1, 7)), dma((ITERS + 1, 7)),
        ],
        compiler_params=pltpu.CompilerParams(
            collective_id=0, has_side_effects=True, vmem_limit_bytes=60 * 1024 * 1024
        ),
    )(vis, flags, positions, lmn, flux, gains, duals)


def solution(mesh):
    finer = Mesh(mesh.devices.reshape(2, 4, mesh.shape["col"], 4, 2), AXES)
    return jax.shard_map(
        shards,
        mesh=finer,
        in_specs=(
            P(BAND, None, None, ROW, "x"),
            P(BAND, None, None),
            P(),
            P(),
            P(BAND, None),
            P(BAND, None, None, None, OWN),
            P(BAND, None, None, None, OWN),
        ),
        out_specs=(P(BAND, None, None, None, OWN), P(BAND, None, None, None, OWN)),
        check_vma=False,
    )
```

```python
import functools
import math

import jax
import jax.numpy as jnp
import numpy as np
from jax import lax
from jax.experimental import pallas as pl
from jax.experimental.pallas import tpu as pltpu
from jax.sharding import Mesh
from jax.sharding import PartitionSpec as P

S = 512
F = 64
ITERS = 2
PENALTY = 0.05
AXES = ("zh", "y", "x", "zl", "core")
BAND = ("zl", "core")
ROW = ("zh", "y")
OWN = ("zh", "y", "x")
MESH = pl.DeviceIdType.MESH
HIGH = lax.Precision.HIGHEST
F32 = jnp.float32
BF16 = jnp.bfloat16
PAIRS = 4
CHUNKS = 1
GATHERS = 2
CROSSED = 3
OWNED = 16
LANES = 128


def fit_polynomials():
    grid = 2.0 * np.arange(F, dtype=np.float64) / (F - 1) - 1.0
    powers = np.stack([grid**k for k in range(4)], axis=1)
    _, upper = np.linalg.qr(powers)
    return np.linalg.inv(upper)


def split(value):
    high = value.astype(BF16)
    return high, (value - high.astype(F32)).astype(BF16)


def kernel(
    vis_hbm, flags_hbm, pos_hbm, lmn_hbm, flux_hbm, gains_hbm, duals_hbm,
    solved,
    vis_buf, flags_ref, pos_ref, lmn_ref, flux_ref, gains_ref, duals_ref, wvis, weight, rmat, lhs, resid,
    row_buf, col_buf, relay_buf, send_buf, num_buf, num_recv,
    t_buf, t_recv, fit_send, fit_recv, sq_send, sq_recv,
    flag_col, flag_row, flag_tmp, flag_far, new_p, far_p, geom_blk, flux_tab,
    in_sem, row_s, row_r, rel_s, rel_r, own_s, fwd_s, col_r,
    num_s, num_r, t_s, t_r, sq_s, sq_r, fit_s, fit_r,
):
    me = {axis: lax.axis_index(axis) for axis in AXES}
    zh, y, x = me["zh"], me["y"], me["x"]

    def at(**moved):
        place = dict(me)
        place.update(moved)
        return tuple(place[axis] for axis in AXES)

    x_peers = [at(x=lax.rem(x + k, 4)) for k in range(1, 4)]
    plane_peers = [
        at(y=lax.rem(y + k // 4, 4), x=lax.rem(x + k % 4, 4)) for k in range(1, 16)
    ]
    line_peers = [
        at(
            zh=lax.rem(zh + k // 8, 2),
            zl=lax.rem(me["zl"] + (k // 2) % 4, 4),
            core=lax.rem(me["core"] + k % 2, 2),
        )
        for k in range(1, 16)
    ]
    band_peers = line_peers[:7]
    plane_order = (9, 8, 10, 5, 13, 7, 1, 6, 4, 14, 12, 0, 2, 3, 11)
    line_order = (7, 8, 9, 10, 11, 12, 13, 14, 3, 4, 5, 6, 1, 2, 0)

    def push(src, dst, send_sem, recv_sem, device):
        return pltpu.make_async_remote_copy(
            src_ref=src, dst_ref=dst, send_sem=send_sem, recv_sem=recv_sem,
            device_id=device, device_id_type=MESH,
        )

    pending = []

    gains_copy, pos_copy, lmn_copy, flux_copy, duals_copy, flags_copy, vis_copy = (
        pltpu.make_async_copy(src, dst, in_sem.at[i])
        for i, (src, dst) in enumerate((
            (gains_hbm, gains_ref), (pos_hbm, pos_ref), (lmn_hbm, lmn_ref),
            (flux_hbm, flux_ref), (duals_hbm, duals_ref), (flags_hbm, flags_ref),
            (vis_hbm, vis_buf),
        ))
    )
    for copy in (gains_copy, pos_copy, lmn_copy, flux_copy, duals_copy, flags_copy, vis_copy):
        copy.start()

    barrier = pltpu.get_barrier_semaphore()
    for peer in [line_peers[k] for k in line_order] + [plane_peers[k] for k in plane_order]:
        pl.semaphore_signal(barrier, inc=1, device_id=peer, device_id_type=MESH)

    lane = lax.broadcasted_iota(jnp.int32, (1, LANES), 1)
    half = lane // 64
    low = lane < 64
    is_im = (lane // 8) % 2 == 1
    sign = jnp.where(is_im, -1.0, 1.0).astype(F32)

    def swapped(value):
        return jnp.where(is_im, pltpu.roll(value, 8, 1), pltpu.roll(value, 120, 1))

    def both(value):
        return value + pltpu.roll(value, 64, 1)

    band = me["zl"] * 2 + me["core"]
    row = zh * 4 + y
    row_block = lax.div(row, 2)
    row_half = pl.multiple_of(lax.rem(row, 2) * 64, 64)
    own_at = pl.multiple_of(lax.rem(row, 2) * 64 + x * OWNED, OWNED)

    dir_hot = (
        lax.broadcasted_iota(jnp.int32, (8, LANES), 0)
        == lax.broadcasted_iota(jnp.int32, (8, LANES), 1) % 8
    ).astype(F32)
    time_of = (lane // 16) % 4
    block = pl.ds(pl.multiple_of(row_block * LANES, LANES), LANES)
    pos_copy.wait()
    lmn_copy.wait()
    lmn_lanes = jnp.dot(lmn_ref[...], dir_hot, precision=HIGH, preferred_element_type=F32)
    places = jnp.concatenate(
        [pos_ref[k, :, block] for k in range(3)] + [jnp.zeros((4, LANES), F32)], axis=0
    ).T
    geom = jnp.zeros((LANES, LANES), F32)
    for t in range(4):
        axis_sum = (
            places[:, t : t + 1] * lmn_lanes[0:1]
            + places[:, t + 4 : t + 5] * lmn_lanes[1:2]
            + places[:, t + 8 : t + 9] * lmn_lanes[2:3]
        )
        geom = jnp.where(time_of == t, axis_sum, geom)
    geom_blk[...] = geom
    geom = geom_blk[pl.ds(own_at, OWNED), :]

    def turned(g, i):
        return g * cos[i] + swapped(g) * sin[i]

    gains_copy.wait()
    cos, sin, gain, dual = [], [], [], []
    for fp in range(PAIRS):
        channel = (8 * band + 2 * fp + half).astype(F32)
        turns = (1.0 + channel / F) * geom
        angle = (2.0 * math.pi) * (turns - jnp.round(turns))
        cos.append(jnp.cos(angle))
        sin.append(sign * jnp.sin(angle))
        gain.append(gains_ref[2 * fp : 2 * fp + 2].reshape(LANES, OWNED).T)
        send_buf[0, fp] = turned(gain[fp], fp)
    duals_copy.wait()
    for fp in range(PAIRS):
        dual.append(duals_ref[2 * fp : 2 * fp + 2].reshape(LANES, OWNED).T)

    inv = fit_polynomials()
    quad = []
    for fp in range(PAIRS):
        channel = (8 * band + 2 * fp + half).astype(F32)
        grid = 2.0 * channel / (F - 1) - 1.0
        square = grid * grid
        quad.append([
            jnp.full((1, LANES), float(inv[0, 0]), F32),
            float(inv[1, 1]) * grid,
            float(inv[2, 2]) * square + float(inv[0, 2]),
            grid * (float(inv[3, 3]) * square + float(inv[1, 3])),
        ])

    def fit_start(stage, g, u):
        total = [g[i] + u[i] for i in range(PAIRS)]
        coef = [
            both(sum(quad[i][k] * total[i] for i in range(PAIRS))) for k in range(4)
        ]
        for j in range(2):
            fit_send[stage, j] = jnp.where(low, coef[2 * j], coef[2 * j + 1])
        for k, peer in enumerate(band_peers):
            copy = push(
                fit_send.at[stage], fit_recv.at[stage, k],
                fit_s.at[stage, k], fit_r.at[stage, k], peer,
            )
            copy.start()
            pending.append(copy)

    def fit_finish(stage):
        for k, peer in enumerate(band_peers):
            push(
                fit_send.at[stage], fit_recv.at[stage, k],
                fit_s.at[stage, k], fit_r.at[stage, k], peer,
            ).wait_recv()
        coef = []
        for j in range(2):
            value = fit_send[stage, j]
            for k in range(7):
                value = value + fit_recv[stage, k, j]
            turn = pltpu.roll(value, 64, 1)
            coef += [jnp.where(low, value, turn), jnp.where(low, turn, value)]
        return [sum(quad[i][k] * coef[k] for k in range(4)) for i in range(PAIRS)]

    own_col = 2 * zh + lax.div(y, 2)
    far_col = 2 * (1 - zh) + lax.div(y, 2)
    slot_rows = pl.ds(pl.multiple_of((lax.rem(y, 2) * 4 + x) * OWNED, OWNED), OWNED)
    x_rows = pl.ds(pl.multiple_of(x * OWNED, OWNED), OWNED)
    near = lax.div(x, 2) == zh

    own_slot = lax.rem(y, 2) * 4 + x

    def part(h):
        return pl.ds(h * (PAIRS // CHUNKS), PAIRS // CHUNKS)

    def across(slot, h):
        return push(
            send_buf.at[slot, part(h)], relay_buf.at[slot, part(h)],
            rel_s.at[slot, h], rel_r.at[slot, h], at(zh=1 - zh),
        )

    def cross(slot):
        for h in range(CHUNKS):
            copy = across(slot, h)
            copy.start()
            pending.append(copy)

    def crossed(slot):
        for h in range(CHUNKS):
            across(slot, h).wait_recv()

    def spread(slot, src):
        copies = []
        for h in range(CHUNKS):
            for k in (2, 1, 3):
                copies.append(push(
                    src.at[part(h)], col_buf.at[slot, part(h), slot_rows],
                    own_s.at[slot, k, h], col_r.at[slot, own_slot, h],
                    at(y=lax.rem(y + k, 4), x=own_col),
                ))
        for copy in copies:
            copy.start()
        pending.extend(copies)

    def spread_row(slot, src):
        for k, peer in enumerate(x_peers):
            copy = push(
                src, row_buf.at[slot, :, x_rows], row_s.at[slot, k], row_r.at[slot, k], peer,
            )
            copy.start()
            pending.append(copy)
        row_buf[slot, :, x_rows, :] = src[...]

    def to_far_col(slot, src, h):
        return push(
            src.at[part(h)], col_buf.at[slot, part(h), slot_rows],
            fwd_s.at[slot, 0, h], col_r.at[slot, own_slot, h], at(x=far_col),
        )

    def relay(slot, src, h):
        for k in range(1, 4):
            copy = push(
                src.at[part(h)], col_buf.at[slot, part(h), slot_rows],
                fwd_s.at[slot, k, h], col_r.at[slot, own_slot, h],
                at(y=lax.rem(y + k, 4), x=far_col),
            )
            copy.start()
            pending.append(copy)

        @pl.when(x != far_col)
        def _():
            to_far_col(slot, src, h).start()

        @pl.when(x == far_col)
        def _():
            col_buf[slot, part(h), slot_rows, :] = src[part(h)]

    def gather_finish(slot, h):
        if h == 0:
            for k, peer in enumerate(x_peers):
                push(
                    new_p, row_buf.at[slot, :, x_rows],
                    row_s.at[slot, k], row_r.at[slot, k], peer,
                ).wait_recv()
        for j in range(8):
            from_y = lax.rem(x, 2) * 2 + j // 4
            rows = slice(OWNED * j, OWNED * (j + 1))
            row_rows = slice(OWNED * (j % 4), OWNED * (j % 4 + 1))
            copy = push(
                new_p.at[part(h)], col_buf.at[slot, part(h), rows],
                own_s.at[slot, 0, h], col_r.at[slot, j, h], x_peers[0],
            )
            arrives = jnp.logical_or(
                from_y != y, jnp.logical_and(jnp.logical_not(near), x != j % 4)
            )

            @pl.when(arrives)
            def _(copy=copy):
                copy.wait_recv()

            @pl.when(jnp.logical_and(from_y == y, near))
            def _(rows=rows, row_rows=row_rows):
                col_buf[slot, part(h), rows, :] = row_buf[slot, part(h), row_rows, :]

    pl.semaphore_wait(barrier, 30)
    cross(0)
    spread(0, send_buf.at[0])
    spread_row(0, send_buf.at[0])
    fit_start(0, gain, dual)

    flux_copy.wait()
    flux_all = jnp.dot(flux_ref[...], dir_hot, precision=HIGH, preferred_element_type=F32)
    for fp in range(PAIRS):
        flux_tab[pl.ds(fp, 1), :] = jnp.where(
            low, flux_all[2 * fp : 2 * fp + 1], flux_all[2 * fp + 1 : 2 * fp + 2]
        )

    pair_hot = (
        lax.broadcasted_iota(jnp.int32, (8, LANES), 0)
        == lax.broadcasted_iota(jnp.int32, (8, LANES), 1) // 16
    ).astype(F32)
    col_block = pl.ds(pl.multiple_of(x * LANES, LANES), LANES)
    far_block = pl.ds(pl.multiple_of(far_col * LANES, LANES), LANES)
    samples = jnp.zeros((4, 1), F32)
    flags_copy.wait()
    for fp in range(PAIRS):
        for place, table in ((col_block, flag_col), (block, flag_row), (far_block, None)):
            live = jnp.concatenate(
                [flags_ref[2 * fp, :, place], flags_ref[2 * fp + 1, :, place]], axis=0
            ).astype(F32)
            table = flag_tmp if table is None else table.at[fp]
            table[...] = lax.dot_general(
                live, pair_hot, (((0,), (0,)), ((), ())), preferred_element_type=F32
            )
        flag_far[fp] = flag_tmp[pl.ds(own_at, OWNED), :]
        for f in (2 * fp, 2 * fp + 1):
            count = jnp.sum(flags_ref[f].astype(F32), axis=1, keepdims=True)
            samples = samples + count * (count - 1.0)
    samples = jnp.sum(samples, axis=0, keepdims=True)

    rmat[...] = jnp.zeros_like(rmat)
    for h in range(CHUNKS):
        across(0, h).wait_recv()
        relay(0, relay_buf.at[0], h)
    smooth = fit_finish(0)
    for i in range(PAIRS):
        send_buf[1, i] = turned(smooth[i] - dual[i], i)
    cross(1)

    vis_copy.wait()
    row_id = row * 64 + lax.broadcasted_iota(jnp.int32, (64, LANES), 0)
    col_id = x * LANES + lax.broadcasted_iota(jnp.int32, (64, LANES), 1)
    distinct = (row_id != col_id).astype(F32)

    def prepare(fp, carry):
        row_flags = flag_row[fp, pl.ds(row_half, 64), :]
        for f2 in range(2):
            f = 2 * fp + f2
            for t in range(4):
                at_lane = 64 * f2 + 16 * t
                w = row_flags[:, at_lane : at_lane + 1] * distinct
                w = w * flags_ref[f, t : t + 1, col_block].astype(F32)
                weight[f, t] = w
                wvis[f, t, :, 0:LANES] = w * vis_buf[f, t, 0].astype(F32)
                wvis[f, t, :, LANES:] = w * vis_buf[f, t, 1].astype(F32)
        return carry

    lax.fori_loop(0, PAIRS, prepare, 0)

    def arrange(it, fp):
        flux = flux_tab[pl.ds(fp, 1), :]
        b = col_buf[it, fp]
        p = row_buf[it, fp]
        b = b * flux
        t_buf[it, pl.ds(fp, 1), :] = jnp.sum(b * b * flag_col[fp], axis=0, keepdims=True)
        turned_b = b.T
        p_high = p.astype(BF16).astype(F32)
        p_low = p - p_high
        for f2 in range(2):
            f = 2 * fp + f2
            for start, value in ((0, p_high), (64, p_low)):
                other = pltpu.roll(value, 64, 1)
                pieces = (value, other) if f2 == 0 else (other, value)
                lhs[f, start : start + 64, :] = jnp.where(low, *pieces).astype(BF16)
            for t in range(4):
                start = 64 * f2 + 16 * t
                left = turned_b[start : start + 16]
                right = jnp.concatenate([-left[8:16], left[0:8]], axis=0)
                high, rest = split(jnp.concatenate([left, right], axis=1))
                rmat[f, t, 16 * t : 16 * t + 16, :] = high
                rmat[f, t, 64 + 16 * t : 64 + 16 * t + 16, :] = rest

    def numerators(it, first, end):
        def pair(fp, carry):
            halves = []
            for f2 in range(2):
                f = 2 * fp + f2
                total = jnp.zeros((LANES, LANES), F32)
                for t in range(4):
                    high, rest = split(resid[f, t])
                    total = total + lax.dot_general(
                        jnp.concatenate([high, rest], axis=0), rmat[f, t],
                        (((1,), (1,)), ((), ())), preferred_element_type=F32,
                    )
                halves.append(both(total[0:64] + total[64:128]))
            num_buf[it, fp] = jnp.where(low, halves[0], halves[1])
            return carry

        lax.fori_loop(first, end, pair, 0, unroll=True)

    def exchange(it, k, peer, there, h):
        rows = pl.ds(pl.multiple_of(there * OWNED, OWNED), OWNED)
        return push(
            num_buf.at[it, part(h), rows], num_recv.at[it, k, part(h)],
            num_s.at[it, k, h], num_r.at[it, k, h], peer,
        )

    def exchange_start(it, h):
        for k, peer in enumerate(x_peers):
            copy = exchange(it, k, peer, lax.rem(x + k + 1, 4), h)
            copy.start()
            pending.append(copy)

    def products(it):
        def residual(f, squares):
            for t in range(4):
                model = jnp.dot(lhs[f], rmat[f, t], preferred_element_type=F32)
                model = model[0:64] + model[64:128]
                w = weight[f, t]
                r = wvis[f, t] - jnp.concatenate([w, w], axis=1) * model
                resid[f, t] = r
                squares = squares + jnp.sum((r * r).reshape(8, 8, 2 * LANES), axis=0)
            return squares

        squares = jnp.zeros((8, 2 * LANES), F32)
        for h in range(CHUNKS):
            gather_finish(it, h)
            first, end = h * PAIRS // CHUNKS, (h + 1) * PAIRS // CHUNKS

            def arranged(fp, carry):
                arrange(it, fp)
                return carry

            lax.fori_loop(first, end, arranged, 0, unroll=True)
            squares = lax.fori_loop(2 * first, 2 * end, residual, squares, unroll=True)
        squares = squares[:, 0:LANES] + squares[:, LANES:]
        return jnp.sum(squares, axis=0, keepdims=True)

    def squares_start(it, stage, value, peers, order):
        sq_send[it, stage] = value
        for k in order:
            peer = peers[k]
            copy = push(
                sq_send.at[it, stage], sq_recv.at[it, stage, k],
                sq_s.at[it, stage, k], sq_r.at[it, stage, k], peer,
            )
            copy.start()
            pending.append(copy)

    def squares_finish(it, stage, peers):
        total = sq_send[it, stage]
        for k, peer in enumerate(peers):
            push(
                sq_send.at[it, stage], sq_recv.at[it, stage, k],
                sq_s.at[it, stage, k], sq_r.at[it, stage, k], peer,
            ).wait_recv()
        for k in range(15):
            total = total + sq_recv[it, stage, k]
        return total

    def exchange_finish(it):
        for k, peer in enumerate(x_peers):
            for h in range(CHUNKS):
                exchange(it, k, peer, x, h).wait_recv()
            push(t_buf.at[it], t_recv.at[it, k], t_s.at[it, k], t_r.at[it, k], peer).wait_recv()
        num = num_buf[it, :, x_rows, :]
        power = t_buf[it]
        for k in range(3):
            num = num + num_recv[it, k]
            power = power + t_recv[it, k]
        power = power + swapped(power)
        return num, power

    def solve_for(p, live, flux, power):
        b = p * flux
        b = b * b
        return live * (power - live * (b + swapped(b)))

    for it in range(ITERS):
        squares = products(it)
        squares_start(it, 0, squares, plane_peers, plane_order)
        for k, peer in enumerate(x_peers):
            copy = push(t_buf.at[it], t_recv.at[it, k], t_s.at[it, k], t_r.at[it, k], peer)
            copy.start()
            pending.append(copy)
        for h in range(CHUNKS):
            numerators(it, h * PAIRS // CHUNKS, (h + 1) * PAIRS // CHUNKS)
            exchange_start(it, h)
        squares = squares_finish(it, 0, plane_peers)
        squares = jnp.sum(squares, axis=1, keepdims=True)
        squares_start(
            it, 1,
            jnp.where(lane == 0, squares, jnp.where(lane == 1, samples, 0.0)),
            line_peers, line_order,
        )
        if it > 0:
            smooth = fit_finish(it)
            dual = [dual[i] + gain[i] - smooth[i] for i in range(PAIRS)]
        num, power = exchange_finish(it)
        if it + 1 < ITERS:
            send_buf[2] = num
            cross(2)
        parts = []
        for i in range(PAIRS):
            target = smooth[i] - dual[i]
            live = flag_row[i, pl.ds(own_at, OWNED), :]
            den = solve_for(
                turned(gain[i], i), live, flux_tab[i : i + 1, :], power[i : i + 1]
            )
            numer = num[i] * cos[i] - swapped(num[i]) * sin[i]
            parts.append((numer + den * gain[i], den, target))
        if it + 1 < ITERS:
            crossed(1)
            far = []
            for i in range(PAIRS):
                p = relay_buf[0, i]
                den = solve_for(p, flag_far[i], flux_tab[i : i + 1, :], power[i : i + 1])
                far.append((p, den, relay_buf[1, i]))
        total = squares_finish(it, 1, line_peers)
        count = 0.5 * jnp.sum(jnp.where(lane == 1, total, 0.0), axis=1, keepdims=True)
        total = jnp.sum(jnp.where(lane == 0, total, 0.0), axis=1, keepdims=True)
        rho = PENALTY * S * (total / count + 1e-06)
        gain = [
            0.5 * (gain[i] + (top + rho * target) / (den + rho))
            for i, (top, den, target) in enumerate(parts)
        ]
        if it + 1 < ITERS:
            for i in range(PAIRS):
                new_p[i] = turned(gain[i], i)
            spread(it + 1, new_p)
            crossed(2)
            for i, (p, den, turn) in enumerate(far):
                far_p[i] = 0.5 * (
                    p + (relay_buf[2, i] + den * p + rho * turn) / (den + rho)
                )
            for h in range(CHUNKS):
                relay(it + 1, far_p, h)
            spread_row(it + 1, new_p)
        fit_start(it + 1, gain, dual)

    for i in range(PAIRS):
        solved[0, i] = gain[i]
    smooth = fit_finish(ITERS)
    for i in range(PAIRS):
        value = dual[i] + gain[i] - smooth[i]
        solved[1, i] = value

    for copy in pending:
        copy.wait_send()

    @pl.when(x != far_col)
    def _():
        for slot in range(GATHERS):
            for h in range(CHUNKS):
                to_far_col(slot, far_p, h).wait_send()


def placed(solved, gains_out, duals_out):
    for k, out in enumerate((gains_out, duals_out)):
        for i in range(PAIRS):
            out[2 * i : 2 * i + 2] = solved[k, i].T.reshape(2, 4, 2, 8, OWNED)


def shards(vis, flags, positions, lmn, flux, gains, duals):
    vmem = pl.BlockSpec(memory_space=pltpu.VMEM)
    positions = jnp.swapaxes(positions, 0, 1)
    dma = pltpu.SemaphoreType.DMA
    solved = pl.pallas_call(
        kernel,
        name="admm",
        out_shape=jax.ShapeDtypeStruct((2, PAIRS, OWNED, LANES), F32),
        in_specs=[pl.BlockSpec(memory_space=pltpu.HBM)] * 7,
        out_specs=vmem,
        scratch_shapes=[
            pltpu.VMEM(vis.shape, BF16),
            pltpu.VMEM(flags.shape, jnp.int32),
            pltpu.VMEM(positions.shape, F32),
            pltpu.VMEM(lmn.shape, F32),
            pltpu.VMEM(flux.shape, F32),
            pltpu.VMEM(gains.shape, F32),
            pltpu.VMEM(duals.shape, F32),
            pltpu.VMEM((8, 4, 64, 2 * LANES), F32),
            pltpu.VMEM((8, 4, 64, LANES), F32),
            pltpu.VMEM((8, 4, LANES, 2 * LANES), BF16),
            pltpu.VMEM((8, LANES, LANES), BF16),
            pltpu.VMEM((8, 4, 64, 2 * LANES), F32),
            pltpu.VMEM((GATHERS, PAIRS, 64, LANES), F32),
            pltpu.VMEM((GATHERS, PAIRS, LANES, LANES), F32),
            pltpu.VMEM((CROSSED, PAIRS, OWNED, LANES), F32),
            pltpu.VMEM((CROSSED, PAIRS, OWNED, LANES), F32),
            pltpu.VMEM((ITERS, PAIRS, 64, LANES), F32),
            pltpu.VMEM((ITERS, 3, PAIRS, OWNED, LANES), F32),
            pltpu.VMEM((ITERS, PAIRS, LANES), F32),
            pltpu.VMEM((ITERS, 3, PAIRS, LANES), F32),
            pltpu.VMEM((ITERS + 1, 2, OWNED, LANES), F32),
            pltpu.VMEM((ITERS + 1, 7, 2, OWNED, LANES), F32),
            pltpu.VMEM((ITERS, 2, 1, LANES), F32),
            pltpu.VMEM((ITERS, 2, 15, 1, LANES), F32),
            pltpu.VMEM((PAIRS, LANES, LANES), F32),
            pltpu.VMEM((PAIRS, LANES, LANES), F32),
            pltpu.VMEM((LANES, LANES), F32),
            pltpu.VMEM((PAIRS, OWNED, LANES), F32),
            pltpu.VMEM((PAIRS, OWNED, LANES), F32),
            pltpu.VMEM((PAIRS, OWNED, LANES), F32),
            pltpu.VMEM((LANES, LANES), F32),
            pltpu.VMEM((PAIRS, LANES), F32),
            dma((7,)),
            dma((GATHERS, 3)), dma((GATHERS, 3)),
            dma((CROSSED, CHUNKS)), dma((CROSSED, CHUNKS)),
            dma((GATHERS, 4, CHUNKS)), dma((GATHERS, 4, CHUNKS)),
            dma((GATHERS, 8, CHUNKS)),
            dma((ITERS, 3, CHUNKS)), dma((ITERS, 3, CHUNKS)),
            dma((ITERS, 3)), dma((ITERS, 3)),
            dma((ITERS, 2, 15)), dma((ITERS, 2, 15)),
            dma((ITERS + 1, 7)), dma((ITERS + 1, 7)),
        ],
        compiler_params=pltpu.CompilerParams(
            collective_id=0, has_side_effects=True, vmem_limit_bytes=60 * 1024 * 1024
        ),
    )(vis, flags, positions, lmn, flux, gains, duals)
    return pl.pallas_call(
        placed,
        name="placed",
        out_shape=(
            jax.ShapeDtypeStruct(gains.shape, F32),
            jax.ShapeDtypeStruct(duals.shape, F32),
        ),
        in_specs=[vmem],
        out_specs=(vmem, vmem),
    )(solved)


def solution(mesh):
    finer = Mesh(mesh.devices.reshape(2, 4, mesh.shape["col"], 4, 2), AXES)
    return jax.shard_map(
        shards,
        mesh=finer,
        in_specs=(
            P(BAND, None, None, ROW, "x"),
            P(BAND, None, None),
            P(),
            P(),
            P(BAND, None),
            P(BAND, None, None, None, OWN),
            P(BAND, None, None, None, OWN),
        ),
        out_specs=(P(BAND, None, None, None, OWN), P(BAND, None, None, None, OWN)),
        check_vma=False,
    )
```

```python
import functools
import math

import jax
import jax.numpy as jnp
import numpy as np
from jax import lax
from jax.experimental import pallas as pl
from jax.experimental.pallas import tpu as pltpu
from jax.sharding import Mesh
from jax.sharding import PartitionSpec as P

S = 512
F = 64
ITERS = 2
PENALTY = 0.05
AXES = ("zh", "y", "x", "zl", "core")
BAND = ("zl", "core")
ROW = ("zh", "y")
OWN = ("zh", "y", "x")
MESH = pl.DeviceIdType.MESH
HIGH = lax.Precision.HIGHEST
F32 = jnp.float32
BF16 = jnp.bfloat16
PAIRS = 4
CHUNKS = 1
GATHERS = 2
CROSSED = 3
OWNED = 16
LANES = 128


def fit_polynomials():
    grid = 2.0 * np.arange(F, dtype=np.float64) / (F - 1) - 1.0
    powers = np.stack([grid**k for k in range(4)], axis=1)
    _, upper = np.linalg.qr(powers)
    return np.linalg.inv(upper)


def split(value):
    high = value.astype(BF16)
    return high, (value - high.astype(F32)).astype(BF16)


def kernel(
    vis_hbm, flags_hbm, pos_hbm, lmn_hbm, flux_hbm, gains_hbm, duals_hbm,
    solved_hbm,
    vis_buf, flags_ref, pos_ref, lmn_ref, flux_ref, gains_ref, duals_ref, wvis, weight, rmat, lhs, resid,
    row_buf, col_buf, relay_buf, send_buf, num_buf, num_recv,
    t_buf, t_recv, fit_send, fit_recv, sq_send, sq_recv,
    flag_col, flag_row, flag_tmp, flag_far, new_p, far_p, geom_blk, flux_tab, solved,
    in_sem, row_s, row_r, rel_s, rel_r, own_s, fwd_s, col_r,
    num_s, num_r, t_s, t_r, sq_s, sq_r, fit_s, fit_r,
):
    me = {axis: lax.axis_index(axis) for axis in AXES}
    zh, y, x = me["zh"], me["y"], me["x"]

    def at(**moved):
        place = dict(me)
        place.update(moved)
        return tuple(place[axis] for axis in AXES)

    x_peers = [at(x=lax.rem(x + k, 4)) for k in range(1, 4)]
    plane_peers = [
        at(y=lax.rem(y + k // 4, 4), x=lax.rem(x + k % 4, 4)) for k in range(1, 16)
    ]
    line_peers = [
        at(
            zh=lax.rem(zh + k // 8, 2),
            zl=lax.rem(me["zl"] + (k // 2) % 4, 4),
            core=lax.rem(me["core"] + k % 2, 2),
        )
        for k in range(1, 16)
    ]
    band_peers = line_peers[:7]
    plane_order = (9, 8, 10, 5, 13, 7, 1, 6, 4, 14, 12, 0, 2, 3, 11)
    line_order = (7, 8, 9, 10, 11, 12, 13, 14, 3, 4, 5, 6, 1, 2, 0)

    def push(src, dst, send_sem, recv_sem, device):
        return pltpu.make_async_remote_copy(
            src_ref=src, dst_ref=dst, send_sem=send_sem, recv_sem=recv_sem,
            device_id=device, device_id_type=MESH,
        )

    pending = []

    def drain(count):
        for copy in pending[:count]:
            copy.wait_send()
        del pending[:count]

    gains_copy, pos_copy, lmn_copy, flux_copy, duals_copy, flags_copy, vis_copy = (
        pltpu.make_async_copy(src, dst, in_sem.at[i])
        for i, (src, dst) in enumerate((
            (gains_hbm, gains_ref), (pos_hbm, pos_ref), (lmn_hbm, lmn_ref),
            (flux_hbm, flux_ref), (duals_hbm, duals_ref), (flags_hbm, flags_ref),
            (vis_hbm, vis_buf),
        ))
    )
    for copy in (gains_copy, pos_copy, lmn_copy, flux_copy, duals_copy, flags_copy, vis_copy):
        copy.start()

    barrier = pltpu.get_barrier_semaphore()
    for peer in [line_peers[k] for k in line_order] + [plane_peers[k] for k in plane_order]:
        pl.semaphore_signal(barrier, inc=1, device_id=peer, device_id_type=MESH)

    lane = lax.broadcasted_iota(jnp.int32, (1, LANES), 1)
    half = lane // 64
    low = lane < 64
    is_im = (lane // 8) % 2 == 1
    sign = jnp.where(is_im, -1.0, 1.0).astype(F32)

    def swapped(value):
        return jnp.where(is_im, pltpu.roll(value, 8, 1), pltpu.roll(value, 120, 1))

    def both(value):
        return value + pltpu.roll(value, 64, 1)

    band = me["zl"] * 2 + me["core"]
    row = zh * 4 + y
    row_block = lax.div(row, 2)
    row_half = pl.multiple_of(lax.rem(row, 2) * 64, 64)
    own_at = pl.multiple_of(lax.rem(row, 2) * 64 + x * OWNED, OWNED)

    dir_hot = (
        lax.broadcasted_iota(jnp.int32, (8, LANES), 0)
        == lax.broadcasted_iota(jnp.int32, (8, LANES), 1) % 8
    ).astype(F32)
    time_of = (lane // 16) % 4
    block = pl.ds(pl.multiple_of(row_block * LANES, LANES), LANES)
    pos_copy.wait()
    lmn_copy.wait()
    lmn_lanes = jnp.dot(lmn_ref[...], dir_hot, precision=HIGH, preferred_element_type=F32)
    places = jnp.concatenate(
        [pos_ref[k, :, block] for k in range(3)] + [jnp.zeros((4, LANES), F32)], axis=0
    ).T
    geom = jnp.zeros((LANES, LANES), F32)
    for t in range(4):
        axis_sum = (
            places[:, t : t + 1] * lmn_lanes[0:1]
            + places[:, t + 4 : t + 5] * lmn_lanes[1:2]
            + places[:, t + 8 : t + 9] * lmn_lanes[2:3]
        )
        geom = jnp.where(time_of == t, axis_sum, geom)
    geom_blk[...] = geom
    geom = geom_blk[pl.ds(own_at, OWNED), :]

    def turned(g, i):
        return g * cos[i] + swapped(g) * sin[i]

    gains_copy.wait()
    cos, sin, gain, dual = [], [], [], []
    for fp in range(PAIRS):
        channel = (8 * band + 2 * fp + half).astype(F32)
        turns = (1.0 + channel / F) * geom
        angle = (2.0 * math.pi) * (turns - jnp.round(turns))
        cos.append(jnp.cos(angle))
        sin.append(sign * jnp.sin(angle))
        gain.append(gains_ref[2 * fp : 2 * fp + 2].reshape(LANES, OWNED).T)
        send_buf[0, fp] = turned(gain[fp], fp)
    duals_copy.wait()
    for fp in range(PAIRS):
        dual.append(duals_ref[2 * fp : 2 * fp + 2].reshape(LANES, OWNED).T)

    inv = fit_polynomials()
    quad = []
    for fp in range(PAIRS):
        channel = (8 * band + 2 * fp + half).astype(F32)
        grid = 2.0 * channel / (F - 1) - 1.0
        square = grid * grid
        quad.append([
            jnp.full((1, LANES), float(inv[0, 0]), F32),
            float(inv[1, 1]) * grid,
            float(inv[2, 2]) * square + float(inv[0, 2]),
            grid * (float(inv[3, 3]) * square + float(inv[1, 3])),
        ])

    def fit_start(stage, g, u):
        total = [g[i] + u[i] for i in range(PAIRS)]
        coef = [
            both(sum(quad[i][k] * total[i] for i in range(PAIRS))) for k in range(4)
        ]
        for j in range(2):
            fit_send[stage, j] = jnp.where(low, coef[2 * j], coef[2 * j + 1])
        for k, peer in enumerate(band_peers):
            copy = push(
                fit_send.at[stage], fit_recv.at[stage, k],
                fit_s.at[stage, k], fit_r.at[stage, k], peer,
            )
            copy.start()
            pending.append(copy)

    def fit_finish(stage):
        for k, peer in enumerate(band_peers):
            push(
                fit_send.at[stage], fit_recv.at[stage, k],
                fit_s.at[stage, k], fit_r.at[stage, k], peer,
            ).wait_recv()
        coef = []
        for j in range(2):
            value = fit_send[stage, j]
            for k in range(7):
                value = value + fit_recv[stage, k, j]
            turn = pltpu.roll(value, 64, 1)
            coef += [jnp.where(low, value, turn), jnp.where(low, turn, value)]
        return [sum(quad[i][k] * coef[k] for k in range(4)) for i in range(PAIRS)]

    own_col = 2 * zh + lax.div(y, 2)
    far_col = 2 * (1 - zh) + lax.div(y, 2)
    slot_rows = pl.ds(pl.multiple_of((lax.rem(y, 2) * 4 + x) * OWNED, OWNED), OWNED)
    x_rows = pl.ds(pl.multiple_of(x * OWNED, OWNED), OWNED)
    near = lax.div(x, 2) == zh

    own_slot = lax.rem(y, 2) * 4 + x

    def part(h):
        return pl.ds(h * (PAIRS // CHUNKS), PAIRS // CHUNKS)

    def across(slot, h):
        return push(
            send_buf.at[slot, part(h)], relay_buf.at[slot, part(h)],
            rel_s.at[slot, h], rel_r.at[slot, h], at(zh=1 - zh),
        )

    def cross(slot):
        for h in range(CHUNKS):
            copy = across(slot, h)
            copy.start()
            pending.append(copy)

    def crossed(slot):
        for h in range(CHUNKS):
            across(slot, h).wait_recv()

    def spread(slot, src):
        copies = [
            push(
                src, col_buf.at[slot, :, slot_rows], own_s.at[slot, k],
                col_r.at[slot, own_slot, 0], at(y=lax.rem(y + k, 4), x=own_col),
            )
            for k in (2, 1, 3)
        ]
        for copy in copies:
            copy.start()
        pending.extend(copies)

    def spread_row(slot, src):
        for k, peer in enumerate(x_peers):
            copy = push(
                src, row_buf.at[slot, :, x_rows], row_s.at[slot, k], row_r.at[slot, k], peer,
            )
            copy.start()
            pending.append(copy)
        row_buf[slot, :, x_rows, :] = src[...]

    def to_far_col(slot, src, h):
        return push(
            src.at[part(h)], col_buf.at[slot, part(h), slot_rows],
            fwd_s.at[slot, 0, h], col_r.at[slot, own_slot, h], at(x=far_col),
        )

    def relay(slot, src, h):
        for k in range(1, 4):
            copy = push(
                src.at[part(h)], col_buf.at[slot, part(h), slot_rows],
                fwd_s.at[slot, k, h], col_r.at[slot, own_slot, h],
                at(y=lax.rem(y + k, 4), x=far_col),
            )
            copy.start()
            pending.append(copy)

        @pl.when(x != far_col)
        def _():
            to_far_col(slot, src, h).start()

        @pl.when(x == far_col)
        def _():
            col_buf[slot, part(h), slot_rows, :] = src[part(h)]

    def gather_finish(slot, h):
        if h == 0:
            for k, peer in enumerate(x_peers):
                push(
                    new_p, row_buf.at[slot, :, x_rows],
                    row_s.at[slot, k], row_r.at[slot, k], peer,
                ).wait_recv()
        for j in range(8):
            from_y = lax.rem(x, 2) * 2 + j // 4
            rows = slice(OWNED * j, OWNED * (j + 1))
            row_rows = slice(OWNED * (j % 4), OWNED * (j % 4 + 1))
            elsewhere = jnp.logical_or(from_y != y, x != j % 4)
            piece = push(
                new_p.at[part(h)], col_buf.at[slot, part(h), rows],
                own_s.at[slot, 0], col_r.at[slot, j, h], x_peers[0],
            )

            @pl.when(jnp.logical_and(jnp.logical_not(near), elsewhere))
            def _(piece=piece):
                piece.wait_recv()

            if h > 0:
                continue
            block = push(
                new_p, col_buf.at[slot, :, rows],
                own_s.at[slot, 0], col_r.at[slot, j, 0], x_peers[0],
            )

            @pl.when(jnp.logical_and(near, from_y != y))
            def _(block=block):
                block.wait_recv()

            @pl.when(jnp.logical_and(near, from_y == y))
            def _(rows=rows, row_rows=row_rows):
                col_buf[slot, :, rows, :] = row_buf[slot, :, row_rows, :]

    pl.semaphore_wait(barrier, 30)
    cross(0)
    spread(0, send_buf.at[0])
    spread_row(0, send_buf.at[0])
    fit_start(0, gain, dual)

    flux_copy.wait()
    flux_all = jnp.dot(flux_ref[...], dir_hot, precision=HIGH, preferred_element_type=F32)
    for fp in range(PAIRS):
        flux_tab[pl.ds(fp, 1), :] = jnp.where(
            low, flux_all[2 * fp : 2 * fp + 1], flux_all[2 * fp + 1 : 2 * fp + 2]
        )

    pair_hot = (
        lax.broadcasted_iota(jnp.int32, (8, LANES), 0)
        == lax.broadcasted_iota(jnp.int32, (8, LANES), 1) // 16
    ).astype(F32)
    col_block = pl.ds(pl.multiple_of(x * LANES, LANES), LANES)
    far_block = pl.ds(pl.multiple_of(far_col * LANES, LANES), LANES)
    samples = jnp.zeros((4, 1), F32)
    flags_copy.wait()
    for fp in range(PAIRS):
        for place, table in ((col_block, flag_col), (block, flag_row), (far_block, None)):
            live = jnp.concatenate(
                [flags_ref[2 * fp, :, place], flags_ref[2 * fp + 1, :, place]], axis=0
            ).astype(F32)
            table = flag_tmp if table is None else table.at[fp]
            table[...] = lax.dot_general(
                live, pair_hot, (((0,), (0,)), ((), ())), preferred_element_type=F32
            )
        flag_far[fp] = flag_tmp[pl.ds(own_at, OWNED), :]
        for f in (2 * fp, 2 * fp + 1):
            count = jnp.sum(flags_ref[f].astype(F32), axis=1, keepdims=True)
            samples = samples + count * (count - 1.0)
    samples = jnp.sum(samples, axis=0, keepdims=True)

    rmat[...] = jnp.zeros_like(rmat)
    for h in range(CHUNKS):
        across(0, h).wait_recv()
        relay(0, relay_buf.at[0], h)
    smooth = fit_finish(0)
    for i in range(PAIRS):
        send_buf[1, i] = turned(smooth[i] - dual[i], i)
    cross(1)

    vis_copy.wait()
    row_id = row * 64 + lax.broadcasted_iota(jnp.int32, (64, LANES), 0)
    col_id = x * LANES + lax.broadcasted_iota(jnp.int32, (64, LANES), 1)
    distinct = (row_id != col_id).astype(F32)

    def prepare(fp, carry):
        row_flags = flag_row[fp, pl.ds(row_half, 64), :]
        for f2 in range(2):
            f = 2 * fp + f2
            for t in range(4):
                at_lane = 64 * f2 + 16 * t
                w = row_flags[:, at_lane : at_lane + 1] * distinct
                w = w * flags_ref[f, t : t + 1, col_block].astype(F32)
                weight[f, t] = w
                wvis[f, t, :, 0:LANES] = w * vis_buf[f, t, 0].astype(F32)
                wvis[f, t, :, LANES:] = w * vis_buf[f, t, 1].astype(F32)
        return carry

    lax.fori_loop(0, PAIRS, prepare, 0)

    def arrange(it, fp):
        flux = flux_tab[pl.ds(fp, 1), :]
        b = col_buf[it, fp]
        p = row_buf[it, fp]
        b = b * flux
        t_buf[it, pl.ds(fp, 1), :] = jnp.sum(b * b * flag_col[fp], axis=0, keepdims=True)
        turned_b = b.T
        p_high = p.astype(BF16).astype(F32)
        p_low = p - p_high
        for f2 in range(2):
            f = 2 * fp + f2
            for start, value in ((0, p_high), (64, p_low)):
                other = pltpu.roll(value, 64, 1)
                pieces = (value, other) if f2 == 0 else (other, value)
                lhs[f, start : start + 64, :] = jnp.where(low, *pieces).astype(BF16)
            for t in range(4):
                start = 64 * f2 + 16 * t
                left = turned_b[start : start + 16]
                right = jnp.concatenate([-left[8:16], left[0:8]], axis=0)
                high, rest = split(jnp.concatenate([left, right], axis=1))
                rmat[f, t, 16 * t : 16 * t + 16, :] = high
                rmat[f, t, 64 + 16 * t : 64 + 16 * t + 16, :] = rest

    def numerators(it, first, end):
        def pair(fp, carry):
            halves = []
            for f2 in range(2):
                f = 2 * fp + f2
                total = jnp.zeros((LANES, LANES), F32)
                for t in range(4):
                    high, rest = split(resid[f, t])
                    total = total + lax.dot_general(
                        jnp.concatenate([high, rest], axis=0), rmat[f, t],
                        (((1,), (1,)), ((), ())), preferred_element_type=F32,
                    )
                halves.append(both(total[0:64] + total[64:128]))
            num_buf[it, fp] = jnp.where(low, halves[0], halves[1])
            return carry

        lax.fori_loop(first, end, pair, 0, unroll=True)

    def exchange(it, k, peer, there):
        rows = pl.ds(pl.multiple_of(there * OWNED, OWNED), OWNED)
        return push(
            num_buf.at[it, :, rows], num_recv.at[it, k],
            num_s.at[it, k], num_r.at[it, k], peer,
        )

    def exchange_start(it):
        for k, peer in enumerate(x_peers):
            copy = exchange(it, k, peer, lax.rem(x + k + 1, 4))
            copy.start()
            pending.append(copy)

    def products(it):
        def residual(f, squares):
            for t in range(4):
                model = jnp.dot(lhs[f], rmat[f, t], preferred_element_type=F32)
                model = model[0:64] + model[64:128]
                w = weight[f, t]
                r = wvis[f, t] - jnp.concatenate([w, w], axis=1) * model
                resid[f, t] = r
                squares = squares + jnp.sum((r * r).reshape(8, 8, 2 * LANES), axis=0)
            return squares

        squares = jnp.zeros((8, 2 * LANES), F32)
        for h in range(CHUNKS):
            gather_finish(it, h)
            first, end = h * PAIRS // CHUNKS, (h + 1) * PAIRS // CHUNKS

            def arranged(fp, carry):
                arrange(it, fp)
                return carry

            lax.fori_loop(first, end, arranged, 0, unroll=True)
            squares = lax.fori_loop(2 * first, 2 * end, residual, squares, unroll=True)
        squares = squares[:, 0:LANES] + squares[:, LANES:]
        return jnp.sum(squares, axis=0, keepdims=True)

    def squares_start(it, stage, value, peers, order):
        sq_send[it, stage] = value
        for k in order:
            peer = peers[k]
            copy = push(
                sq_send.at[it, stage], sq_recv.at[it, stage, k],
                sq_s.at[it, stage, k], sq_r.at[it, stage, k], peer,
            )
            copy.start()
            pending.append(copy)

    def squares_finish(it, stage, peers):
        total = sq_send[it, stage]
        for k, peer in enumerate(peers):
            push(
                sq_send.at[it, stage], sq_recv.at[it, stage, k],
                sq_s.at[it, stage, k], sq_r.at[it, stage, k], peer,
            ).wait_recv()
        for k in range(15):
            total = total + sq_recv[it, stage, k]
        return total

    def exchange_finish(it):
        for k, peer in enumerate(x_peers):
            exchange(it, k, peer, x).wait_recv()
            push(t_buf.at[it], t_recv.at[it, k], t_s.at[it, k], t_r.at[it, k], peer).wait_recv()
        num = num_buf[it, :, x_rows, :]
        power = t_buf[it]
        for k in range(3):
            num = num + num_recv[it, k]
            power = power + t_recv[it, k]
        power = power + swapped(power)
        return num, power

    def solve_for(p, live, flux, power):
        b = p * flux
        b = b * b
        return live * (power - live * (b + swapped(b)))

    for it in range(ITERS):
        squares = products(it)
        squares_start(it, 0, squares, plane_peers, plane_order)
        for k, peer in enumerate(x_peers):
            copy = push(t_buf.at[it], t_recv.at[it, k], t_s.at[it, k], t_r.at[it, k], peer)
            copy.start()
            pending.append(copy)
        numerators(it, 0, PAIRS)
        exchange_start(it)
        squares = squares_finish(it, 0, plane_peers)
        squares = jnp.sum(squares, axis=1, keepdims=True)
        started = len(pending)
        squares_start(
            it, 1,
            jnp.where(lane == 0, squares, jnp.where(lane == 1, samples, 0.0)),
            line_peers, line_order,
        )
        if it > 0:
            smooth = fit_finish(it)
            dual = [dual[i] + gain[i] - smooth[i] for i in range(PAIRS)]
        num, power = exchange_finish(it)
        if it + 1 < ITERS:
            send_buf[2] = num
            cross(2)
        parts = []
        for i in range(PAIRS):
            target = smooth[i] - dual[i]
            live = flag_row[i, pl.ds(own_at, OWNED), :]
            den = solve_for(
                turned(gain[i], i), live, flux_tab[i : i + 1, :], power[i : i + 1]
            )
            numer = num[i] * cos[i] - swapped(num[i]) * sin[i]
            parts.append((numer + den * gain[i], den, target))
        if it + 1 < ITERS:
            crossed(1)
            far = []
            for i in range(PAIRS):
                p = relay_buf[0, i]
                den = solve_for(p, flag_far[i], flux_tab[i : i + 1, :], power[i : i + 1])
                far.append((p, den, relay_buf[1, i]))
        drain(started)
        total = squares_finish(it, 1, line_peers)
        count = 0.5 * jnp.sum(jnp.where(lane == 1, total, 0.0), axis=1, keepdims=True)
        total = jnp.sum(jnp.where(lane == 0, total, 0.0), axis=1, keepdims=True)
        rho = PENALTY * S * (total / count + 1e-06)
        gain = [
            0.5 * (gain[i] + (top + rho * target) / (den + rho))
            for i, (top, den, target) in enumerate(parts)
        ]
        if it + 1 < ITERS:
            for i in range(PAIRS):
                new_p[i] = turned(gain[i], i)
            spread(it + 1, new_p)
            crossed(2)
            for i, (p, den, turn) in enumerate(far):
                far_p[i] = 0.5 * (
                    p + (relay_buf[2, i] + den * p + rho * turn) / (den + rho)
                )
            for h in range(CHUNKS):
                relay(it + 1, far_p, h)
            spread_row(it + 1, new_p)
        started = len(pending)
        fit_start(it + 1, gain, dual)

    for i in range(PAIRS):
        solved[0, i] = gain[i]
    keep_gain = pltpu.make_async_copy(solved.at[0], solved_hbm.at[0], in_sem.at[7])
    keep_gain.start()
    drain(started)

    @pl.when(x != far_col)
    def _():
        for slot in range(GATHERS):
            for h in range(CHUNKS):
                to_far_col(slot, far_p, h).wait_send()

    smooth = fit_finish(ITERS)
    for i in range(PAIRS):
        value = dual[i] + gain[i] - smooth[i]
        solved[1, i] = value
    keep_dual = pltpu.make_async_copy(solved.at[1], solved_hbm.at[1], in_sem.at[8])
    keep_dual.start()

    drain(len(pending))
    keep_gain.wait()
    keep_dual.wait()


def placed(solved, gains_out, duals_out, dense, laid, in_sem, out_sem):
    loads = [
        pltpu.make_async_copy(solved.at[k], dense.at[k], in_sem.at[k]) for k in range(2)
    ]
    for load in loads:
        load.start()
    stores = []
    for k, out in enumerate((gains_out, duals_out)):
        loads[k].wait()
        for i in range(PAIRS):
            laid[k, 2 * i : 2 * i + 2] = dense[k, i].T.reshape(2, 4, 2, 8, OWNED)
        stores.append(pltpu.make_async_copy(laid.at[k], out, out_sem.at[k]))
        stores[k].start()
    for store in stores:
        store.wait()


def shards(vis, flags, positions, lmn, flux, gains, duals):
    hbm = pl.BlockSpec(memory_space=pltpu.HBM)
    positions = jnp.swapaxes(positions, 0, 1)
    dma = pltpu.SemaphoreType.DMA
    solved = pl.pallas_call(
        kernel,
        name="admm",
        out_shape=jax.ShapeDtypeStruct((2, PAIRS, OWNED, LANES), F32),
        in_specs=[pl.BlockSpec(memory_space=pltpu.HBM)] * 7,
        out_specs=hbm,
        scratch_shapes=[
            pltpu.VMEM(vis.shape, BF16),
            pltpu.VMEM(flags.shape, jnp.int32),
            pltpu.VMEM(positions.shape, F32),
            pltpu.VMEM(lmn.shape, F32),
            pltpu.VMEM(flux.shape, F32),
            pltpu.VMEM(gains.shape, F32),
            pltpu.VMEM(duals.shape, F32),
            pltpu.VMEM((8, 4, 64, 2 * LANES), F32),
            pltpu.VMEM((8, 4, 64, LANES), F32),
            pltpu.VMEM((8, 4, LANES, 2 * LANES), BF16),
            pltpu.VMEM((8, LANES, LANES), BF16),
            pltpu.VMEM((8, 4, 64, 2 * LANES), F32),
            pltpu.VMEM((GATHERS, PAIRS, 64, LANES), F32),
            pltpu.VMEM((GATHERS, PAIRS, LANES, LANES), F32),
            pltpu.VMEM((CROSSED, PAIRS, OWNED, LANES), F32),
            pltpu.VMEM((CROSSED, PAIRS, OWNED, LANES), F32),
            pltpu.VMEM((ITERS, PAIRS, 64, LANES), F32),
            pltpu.VMEM((ITERS, 3, PAIRS, OWNED, LANES), F32),
            pltpu.VMEM((ITERS, PAIRS, LANES), F32),
            pltpu.VMEM((ITERS, 3, PAIRS, LANES), F32),
            pltpu.VMEM((ITERS + 1, 2, OWNED, LANES), F32),
            pltpu.VMEM((ITERS + 1, 7, 2, OWNED, LANES), F32),
            pltpu.VMEM((ITERS, 2, 1, LANES), F32),
            pltpu.VMEM((ITERS, 2, 15, 1, LANES), F32),
            pltpu.VMEM((PAIRS, LANES, LANES), F32),
            pltpu.VMEM((PAIRS, LANES, LANES), F32),
            pltpu.VMEM((LANES, LANES), F32),
            pltpu.VMEM((PAIRS, OWNED, LANES), F32),
            pltpu.VMEM((PAIRS, OWNED, LANES), F32),
            pltpu.VMEM((PAIRS, OWNED, LANES), F32),
            pltpu.VMEM((LANES, LANES), F32),
            pltpu.VMEM((PAIRS, LANES), F32),
            pltpu.VMEM((2, PAIRS, OWNED, LANES), F32),
            dma((9,)),
            dma((GATHERS, 3)), dma((GATHERS, 3)),
            dma((CROSSED, CHUNKS)), dma((CROSSED, CHUNKS)),
            dma((GATHERS, 4)), dma((GATHERS, 4, CHUNKS)),
            dma((GATHERS, 8, CHUNKS)),
            dma((ITERS, 3)), dma((ITERS, 3)),
            dma((ITERS, 3)), dma((ITERS, 3)),
            dma((ITERS, 2, 15)), dma((ITERS, 2, 15)),
            dma((ITERS + 1, 7)), dma((ITERS + 1, 7)),
        ],
        compiler_params=pltpu.CompilerParams(
            collective_id=0, has_side_effects=True, vmem_limit_bytes=60 * 1024 * 1024
        ),
    )(vis, flags, positions, lmn, flux, gains, duals)
    return pl.pallas_call(
        placed,
        name="placed",
        out_shape=(
            jax.ShapeDtypeStruct(gains.shape, F32),
            jax.ShapeDtypeStruct(duals.shape, F32),
        ),
        in_specs=[hbm],
        out_specs=(hbm, hbm),
        scratch_shapes=[
            pltpu.VMEM((2, PAIRS, OWNED, LANES), F32),
            pltpu.VMEM((2, *gains.shape), F32),
            dma((2,)), dma((2,)),
        ],
    )(solved)


def solution(mesh):
    finer = Mesh(mesh.devices.reshape(2, 4, mesh.shape["col"], 4, 2), AXES)
    return jax.shard_map(
        shards,
        mesh=finer,
        in_specs=(
            P(BAND, None, None, ROW, "x"),
            P(BAND, None, None),
            P(),
            P(),
            P(BAND, None),
            P(BAND, None, None, None, OWN),
            P(BAND, None, None, None, OWN),
        ),
        out_specs=(P(BAND, None, None, None, OWN), P(BAND, None, None, None, OWN)),
        check_vma=False,
    )
```

```python
import functools
import math

import jax
import jax.numpy as jnp
import numpy as np
from jax import lax
from jax.experimental import pallas as pl
from jax.experimental.pallas import tpu as pltpu
from jax.sharding import Mesh
from jax.sharding import PartitionSpec as P

S = 512
F = 64
ITERS = 2
PENALTY = 0.05
AXES = ("zh", "y", "x", "zl", "core")
BAND = ("zl", "core")
ROW = ("zh", "y")
OWN = ("zh", "y", "x")
MESH = pl.DeviceIdType.MESH
HIGH = lax.Precision.HIGHEST
F32 = jnp.float32
BF16 = jnp.bfloat16
PAIRS = 4
CHUNKS = 1
GATHERS = 2
CROSSED = 3
OWNED = 16
LANES = 128


def fit_polynomials():
    grid = 2.0 * np.arange(F, dtype=np.float64) / (F - 1) - 1.0
    powers = np.stack([grid**k for k in range(4)], axis=1)
    _, upper = np.linalg.qr(powers)
    return np.linalg.inv(upper)


def split(value):
    high = value.astype(BF16)
    return high, (value - high.astype(F32)).astype(BF16)


def kernel(
    vis_hbm, flags_hbm, pos_hbm, lmn_hbm, flux_hbm, gains_hbm, duals_hbm,
    solved_hbm,
    vis_buf, flags_ref, pos_ref, lmn_ref, flux_ref, gains_ref, duals_ref, wvis, weight, rmat, lhs, resid,
    row_buf, col_buf, relay_buf, send_buf, num_buf, num_recv,
    t_buf, t_recv, fit_send, fit_recv, sq_send, sq_recv,
    flag_col, flag_row, flag_tmp, flag_far, new_p, far_p, geom_blk, flux_tab, solved,
    in_sem, row_s, row_r, rel_s, rel_r, own_s, fwd_s, col_r,
    num_s, num_r, t_s, t_r, sq_s, sq_r, fit_s, fit_r,
):
    me = {axis: lax.axis_index(axis) for axis in AXES}
    zh, y, x = me["zh"], me["y"], me["x"]

    def at(**moved):
        place = dict(me)
        place.update(moved)
        return tuple(place[axis] for axis in AXES)

    x_peers = [at(x=lax.rem(x + k, 4)) for k in range(1, 4)]
    plane_peers = [
        at(y=lax.rem(y + k // 4, 4), x=lax.rem(x + k % 4, 4)) for k in range(1, 16)
    ]
    line_peers = [
        at(
            zh=lax.rem(zh + k // 8, 2),
            zl=lax.rem(me["zl"] + (k // 2) % 4, 4),
            core=lax.rem(me["core"] + k % 2, 2),
        )
        for k in range(1, 16)
    ]
    band_peers = line_peers[:7]
    plane_order = (9, 8, 10, 5, 13, 7, 1, 6, 4, 14, 12, 0, 2, 3, 11)
    line_order = (7, 8, 9, 10, 11, 12, 13, 14, 3, 4, 5, 6, 1, 2, 0)

    def push(src, dst, send_sem, recv_sem, device):
        return pltpu.make_async_remote_copy(
            src_ref=src, dst_ref=dst, send_sem=send_sem, recv_sem=recv_sem,
            device_id=device, device_id_type=MESH,
        )

    pending = []

    def drain(count):
        for copy in pending[:count]:
            copy.wait_send()
        del pending[:count]

    gains_copy, pos_copy, lmn_copy, flux_copy, duals_copy, flags_copy, vis_copy = (
        pltpu.make_async_copy(src, dst, in_sem.at[i])
        for i, (src, dst) in enumerate((
            (gains_hbm, gains_ref), (pos_hbm, pos_ref), (lmn_hbm, lmn_ref),
            (flux_hbm, flux_ref), (duals_hbm, duals_ref), (flags_hbm, flags_ref),
            (vis_hbm, vis_buf),
        ))
    )
    for copy in (gains_copy, pos_copy, lmn_copy, flux_copy, duals_copy, flags_copy, vis_copy):
        copy.start()

    barrier = pltpu.get_barrier_semaphore()
    for peer in [line_peers[k] for k in line_order] + [plane_peers[k] for k in plane_order]:
        pl.semaphore_signal(barrier, inc=1, device_id=peer, device_id_type=MESH)

    lane = lax.broadcasted_iota(jnp.int32, (1, LANES), 1)
    half = lane // 64
    low = lane < 64
    is_im = (lane // 8) % 2 == 1
    sign = jnp.where(is_im, -1.0, 1.0).astype(F32)

    def swapped(value):
        return jnp.where(is_im, pltpu.roll(value, 8, 1), pltpu.roll(value, 120, 1))

    def both(value):
        return value + pltpu.roll(value, 64, 1)

    band = me["zl"] * 2 + me["core"]
    row = zh * 4 + y
    row_block = lax.div(row, 2)
    row_half = pl.multiple_of(lax.rem(row, 2) * 64, 64)
    own_at = pl.multiple_of(lax.rem(row, 2) * 64 + x * OWNED, OWNED)

    dir_hot = (
        lax.broadcasted_iota(jnp.int32, (8, LANES), 0)
        == lax.broadcasted_iota(jnp.int32, (8, LANES), 1) % 8
    ).astype(F32)
    time_of = (lane // 16) % 4
    block = pl.ds(pl.multiple_of(row_block * LANES, LANES), LANES)
    pos_copy.wait()
    lmn_copy.wait()
    lmn_lanes = jnp.dot(lmn_ref[...], dir_hot, precision=HIGH, preferred_element_type=F32)
    places = jnp.concatenate(
        [pos_ref[k, :, block] for k in range(3)] + [jnp.zeros((4, LANES), F32)], axis=0
    ).T
    geom = jnp.zeros((LANES, LANES), F32)
    for t in range(4):
        axis_sum = (
            places[:, t : t + 1] * lmn_lanes[0:1]
            + places[:, t + 4 : t + 5] * lmn_lanes[1:2]
            + places[:, t + 8 : t + 9] * lmn_lanes[2:3]
        )
        geom = jnp.where(time_of == t, axis_sum, geom)
    geom_blk[...] = geom
    geom = geom_blk[pl.ds(own_at, OWNED), :]

    def turned(g, i):
        return g * cos[i] + swapped(g) * sin[i]

    gains_copy.wait()
    cos, sin, gain, dual = [], [], [], []
    for fp in range(PAIRS):
        channel = (8 * band + 2 * fp + half).astype(F32)
        turns = (1.0 + channel / F) * geom
        angle = (2.0 * math.pi) * (turns - jnp.round(turns))
        cos.append(jnp.cos(angle))
        sin.append(sign * jnp.sin(angle))
        gain.append(gains_ref[2 * fp : 2 * fp + 2].reshape(LANES, OWNED).T)
        send_buf[0, fp] = turned(gain[fp], fp)
    duals_copy.wait()
    for fp in range(PAIRS):
        dual.append(duals_ref[2 * fp : 2 * fp + 2].reshape(LANES, OWNED).T)

    inv = fit_polynomials()
    quad = []
    for fp in range(PAIRS):
        channel = (8 * band + 2 * fp + half).astype(F32)
        grid = 2.0 * channel / (F - 1) - 1.0
        square = grid * grid
        quad.append([
            jnp.full((1, LANES), float(inv[0, 0]), F32),
            float(inv[1, 1]) * grid,
            float(inv[2, 2]) * square + float(inv[0, 2]),
            grid * (float(inv[3, 3]) * square + float(inv[1, 3])),
        ])

    def fit_start(stage, g, u):
        total = [g[i] + u[i] for i in range(PAIRS)]
        coef = [
            both(sum(quad[i][k] * total[i] for i in range(PAIRS))) for k in range(4)
        ]
        for j in range(2):
            fit_send[stage, j] = jnp.where(low, coef[2 * j], coef[2 * j + 1])
        for k, peer in enumerate(band_peers):
            copy = push(
                fit_send.at[stage], fit_recv.at[stage, k],
                fit_s.at[stage, k], fit_r.at[stage, k], peer,
            )
            copy.start()
            pending.append(copy)

    def fit_finish(stage):
        for k, peer in enumerate(band_peers):
            push(
                fit_send.at[stage], fit_recv.at[stage, k],
                fit_s.at[stage, k], fit_r.at[stage, k], peer,
            ).wait_recv()
        coef = []
        for j in range(2):
            value = fit_send[stage, j]
            for k in range(7):
                value = value + fit_recv[stage, k, j]
            turn = pltpu.roll(value, 64, 1)
            coef += [jnp.where(low, value, turn), jnp.where(low, turn, value)]
        return [sum(quad[i][k] * coef[k] for k in range(4)) for i in range(PAIRS)]

    own_col = 2 * zh + lax.div(y, 2)
    far_col = 2 * (1 - zh) + lax.div(y, 2)
    slot_rows = pl.ds(pl.multiple_of((lax.rem(y, 2) * 4 + x) * OWNED, OWNED), OWNED)
    x_rows = pl.ds(pl.multiple_of(x * OWNED, OWNED), OWNED)
    near = lax.div(x, 2) == zh

    own_slot = lax.rem(y, 2) * 4 + x

    def part(h):
        return pl.ds(h * (PAIRS // CHUNKS), PAIRS // CHUNKS)

    def across(slot, h):
        return push(
            send_buf.at[slot, part(h)], relay_buf.at[slot, part(h)],
            rel_s.at[slot, h], rel_r.at[slot, h], at(zh=1 - zh),
        )

    def cross(slot):
        for h in range(CHUNKS):
            copy = across(slot, h)
            copy.start()
            pending.append(copy)

    def crossed(slot):
        for h in range(CHUNKS):
            across(slot, h).wait_recv()

    def spread(slot, src):
        copies = [
            push(
                src, col_buf.at[slot, :, slot_rows], own_s.at[slot, k],
                col_r.at[slot, own_slot, 0], at(y=lax.rem(y + k, 4), x=own_col),
            )
            for k in (2, 1, 3)
        ]
        for copy in copies:
            copy.start()
        pending.extend(copies)

    def spread_row(slot, src):
        for k, peer in enumerate(x_peers):
            copy = push(
                src, row_buf.at[slot, :, x_rows], row_s.at[slot, k], row_r.at[slot, k], peer,
            )
            copy.start()
            pending.append(copy)
        row_buf[slot, :, x_rows, :] = src[...]

    def to_far_col(slot, src, h):
        return push(
            src.at[part(h)], col_buf.at[slot, part(h), slot_rows],
            fwd_s.at[slot, 0, h], col_r.at[slot, own_slot, h], at(x=far_col),
        )

    def relay(slot, src, h):
        for k in range(1, 4):
            copy = push(
                src.at[part(h)], col_buf.at[slot, part(h), slot_rows],
                fwd_s.at[slot, k, h], col_r.at[slot, own_slot, h],
                at(y=lax.rem(y + k, 4), x=far_col),
            )
            copy.start()
            pending.append(copy)

        @pl.when(x != far_col)
        def _():
            to_far_col(slot, src, h).start()

        @pl.when(x == far_col)
        def _():
            col_buf[slot, part(h), slot_rows, :] = src[part(h)]

    def gather_finish(slot, h):
        if h == 0:
            for k, peer in enumerate(x_peers):
                push(
                    new_p, row_buf.at[slot, :, x_rows],
                    row_s.at[slot, k], row_r.at[slot, k], peer,
                ).wait_recv()
        for j in range(8):
            from_y = lax.rem(x, 2) * 2 + j // 4
            rows = slice(OWNED * j, OWNED * (j + 1))
            row_rows = slice(OWNED * (j % 4), OWNED * (j % 4 + 1))
            elsewhere = jnp.logical_or(from_y != y, x != j % 4)
            piece = push(
                new_p.at[part(h)], col_buf.at[slot, part(h), rows],
                own_s.at[slot, 0], col_r.at[slot, j, h], x_peers[0],
            )

            @pl.when(jnp.logical_and(jnp.logical_not(near), elsewhere))
            def _(piece=piece):
                piece.wait_recv()

            if h > 0:
                continue
            block = push(
                new_p, col_buf.at[slot, :, rows],
                own_s.at[slot, 0], col_r.at[slot, j, 0], x_peers[0],
            )

            @pl.when(jnp.logical_and(near, from_y != y))
            def _(block=block):
                block.wait_recv()

            @pl.when(jnp.logical_and(near, from_y == y))
            def _(rows=rows, row_rows=row_rows):
                col_buf[slot, :, rows, :] = row_buf[slot, :, row_rows, :]

    pl.semaphore_wait(barrier, 30)
    cross(0)
    spread(0, send_buf.at[0])
    spread_row(0, send_buf.at[0])
    fit_start(0, gain, dual)

    flux_copy.wait()
    flux_all = jnp.dot(flux_ref[...], dir_hot, precision=HIGH, preferred_element_type=F32)
    for fp in range(PAIRS):
        flux_tab[pl.ds(fp, 1), :] = jnp.where(
            low, flux_all[2 * fp : 2 * fp + 1], flux_all[2 * fp + 1 : 2 * fp + 2]
        )

    pair_hot = (
        lax.broadcasted_iota(jnp.int32, (8, LANES), 0)
        == lax.broadcasted_iota(jnp.int32, (8, LANES), 1) // 16
    ).astype(F32)
    col_block = pl.ds(pl.multiple_of(x * LANES, LANES), LANES)
    far_block = pl.ds(pl.multiple_of(far_col * LANES, LANES), LANES)
    samples = jnp.zeros((4, 1), F32)
    flags_copy.wait()
    for fp in range(PAIRS):
        for place, table in ((col_block, flag_col), (block, flag_row), (far_block, None)):
            live = jnp.concatenate(
                [flags_ref[2 * fp, :, place], flags_ref[2 * fp + 1, :, place]], axis=0
            ).astype(F32)
            table = flag_tmp if table is None else table.at[fp]
            table[...] = lax.dot_general(
                live, pair_hot, (((0,), (0,)), ((), ())), preferred_element_type=F32
            )
        flag_far[fp] = flag_tmp[pl.ds(own_at, OWNED), :]
        for f in (2 * fp, 2 * fp + 1):
            count = jnp.sum(flags_ref[f].astype(F32), axis=1, keepdims=True)
            samples = samples + count * (count - 1.0)
    samples = jnp.sum(samples, axis=0, keepdims=True)

    rmat[...] = jnp.zeros_like(rmat)
    for h in range(CHUNKS):
        across(0, h).wait_recv()
        relay(0, relay_buf.at[0], h)
    smooth = fit_finish(0)
    for i in range(PAIRS):
        send_buf[1, i] = turned(smooth[i] - dual[i], i)
    cross(1)

    vis_copy.wait()
    row_id = row * 64 + lax.broadcasted_iota(jnp.int32, (64, LANES), 0)
    col_id = x * LANES + lax.broadcasted_iota(jnp.int32, (64, LANES), 1)
    distinct = (row_id != col_id).astype(F32)

    def prepare(fp, carry):
        row_flags = flag_row[fp, pl.ds(row_half, 64), :]
        for f2 in range(2):
            f = 2 * fp + f2
            for t in range(4):
                at_lane = 64 * f2 + 16 * t
                w = row_flags[:, at_lane : at_lane + 1] * distinct
                w = w * flags_ref[f, t : t + 1, col_block].astype(F32)
                weight[f, t] = w
                wvis[f, t, :, 0:LANES] = w * vis_buf[f, t, 0].astype(F32)
                wvis[f, t, :, LANES:] = w * vis_buf[f, t, 1].astype(F32)
        return carry

    lax.fori_loop(0, PAIRS, prepare, 0)

    def arrange(it, fp):
        flux = flux_tab[pl.ds(fp, 1), :]
        b = col_buf[it, fp]
        p = row_buf[it, fp]
        b = b * flux
        t_buf[it, pl.ds(fp, 1), :] = jnp.sum(b * b * flag_col[fp], axis=0, keepdims=True)
        turned_b = b.T
        p_high = p.astype(BF16).astype(F32)
        p_low = p - p_high
        for f2 in range(2):
            f = 2 * fp + f2
            for start, value in ((0, p_high), (64, p_low)):
                other = pltpu.roll(value, 64, 1)
                pieces = (value, other) if f2 == 0 else (other, value)
                if start > 0:
                    pieces = (pieces[0], 0.0)
                lhs[f, :, 2 * start : 2 * start + LANES] = jnp.where(low, *pieces).astype(BF16)
            for t in range(4):
                start = 64 * f2 + 16 * t
                left = turned_b[start : start + 16]
                right = jnp.concatenate([-left[8:16], left[0:8]], axis=0)
                high, rest = split(jnp.concatenate([left, right], axis=1))
                rmat[f, t, 16 * t : 16 * t + 16, :] = high
                rmat[f, t, 64 + 16 * t : 64 + 16 * t + 16, :] = rest
                rmat[f, t, 128 + 16 * t : 128 + 16 * t + 16, :] = high

    def numerators(it, first, end):
        def pair(fp, carry):
            halves = []
            for f2 in range(2):
                f = 2 * fp + f2
                total = jnp.zeros((LANES, LANES), F32)
                for t in range(4):
                    high, rest = split(resid[f, t])
                    total = total + lax.dot_general(
                        jnp.concatenate([high, rest], axis=0), rmat[f, t, 0:LANES, :],
                        (((1,), (1,)), ((), ())), preferred_element_type=F32,
                    )
                halves.append(both(total[0:64] + total[64:128]))
            num_buf[it, fp] = jnp.where(low, halves[0], halves[1])
            return carry

        lax.fori_loop(first, end, pair, 0, unroll=True)

    def exchange(it, k, peer, there):
        rows = pl.ds(pl.multiple_of(there * OWNED, OWNED), OWNED)
        return push(
            num_buf.at[it, :, rows], num_recv.at[it, k],
            num_s.at[it, k], num_r.at[it, k], peer,
        )

    def exchange_start(it):
        for k, peer in enumerate(x_peers):
            copy = exchange(it, k, peer, lax.rem(x + k + 1, 4))
            copy.start()
            pending.append(copy)

    def products(it):
        def residual(f, squares):
            for t in range(4):
                model = jnp.dot(lhs[f], rmat[f, t], preferred_element_type=F32)
                w = weight[f, t]
                r = wvis[f, t] - jnp.concatenate([w, w], axis=1) * model
                resid[f, t] = r
                squares = squares + jnp.sum((r * r).reshape(8, 8, 2 * LANES), axis=0)
            return squares

        squares = jnp.zeros((8, 2 * LANES), F32)
        for h in range(CHUNKS):
            gather_finish(it, h)
            first, end = h * PAIRS // CHUNKS, (h + 1) * PAIRS // CHUNKS

            def arranged(fp, carry):
                arrange(it, fp)
                return carry

            lax.fori_loop(first, end, arranged, 0, unroll=True)
            squares = lax.fori_loop(2 * first, 2 * end, residual, squares, unroll=True)
        squares = squares[:, 0:LANES] + squares[:, LANES:]
        return jnp.sum(squares, axis=0, keepdims=True)

    def squares_start(it, stage, value, peers, order):
        sq_send[it, stage] = value
        for k in order:
            peer = peers[k]
            copy = push(
                sq_send.at[it, stage], sq_recv.at[it, stage, k],
                sq_s.at[it, stage, k], sq_r.at[it, stage, k], peer,
            )
            copy.start()
            pending.append(copy)

    def squares_finish(it, stage, peers):
        total = sq_send[it, stage]
        for k, peer in enumerate(peers):
            push(
                sq_send.at[it, stage], sq_recv.at[it, stage, k],
                sq_s.at[it, stage, k], sq_r.at[it, stage, k], peer,
            ).wait_recv()
        for k in range(15):
            total = total + sq_recv[it, stage, k]
        return total

    def exchange_finish(it):
        for k, peer in enumerate(x_peers):
            exchange(it, k, peer, x).wait_recv()
            push(t_buf.at[it], t_recv.at[it, k], t_s.at[it, k], t_r.at[it, k], peer).wait_recv()
        num = num_buf[it, :, x_rows, :]
        power = t_buf[it]
        for k in range(3):
            num = num + num_recv[it, k]
            power = power + t_recv[it, k]
        power = power + swapped(power)
        return num, power

    def solve_for(p, live, flux, power):
        b = p * flux
        b = b * b
        return live * (power - live * (b + swapped(b)))

    for it in range(ITERS):
        squares = products(it)
        squares_start(it, 0, squares, plane_peers, plane_order)
        for k, peer in enumerate(x_peers):
            copy = push(t_buf.at[it], t_recv.at[it, k], t_s.at[it, k], t_r.at[it, k], peer)
            copy.start()
            pending.append(copy)
        numerators(it, 0, PAIRS)
        exchange_start(it)
        squares = squares_finish(it, 0, plane_peers)
        squares = jnp.sum(squares, axis=1, keepdims=True)
        started = len(pending)
        squares_start(
            it, 1,
            jnp.where(lane == 0, squares, jnp.where(lane == 1, samples, 0.0)),
            line_peers, line_order,
        )
        if it > 0:
            smooth = fit_finish(it)
            dual = [dual[i] + gain[i] - smooth[i] for i in range(PAIRS)]
        num, power = exchange_finish(it)
        if it + 1 < ITERS:
            send_buf[2] = num
            cross(2)
        parts = []
        for i in range(PAIRS):
            target = smooth[i] - dual[i]
            live = flag_row[i, pl.ds(own_at, OWNED), :]
            den = solve_for(
                turned(gain[i], i), live, flux_tab[i : i + 1, :], power[i : i + 1]
            )
            numer = num[i] * cos[i] - swapped(num[i]) * sin[i]
            parts.append((numer + den * gain[i], den, target))
        if it + 1 < ITERS:
            crossed(1)
            far = []
            for i in range(PAIRS):
                p = relay_buf[0, i]
                den = solve_for(p, flag_far[i], flux_tab[i : i + 1, :], power[i : i + 1])
                far.append((p, den, relay_buf[1, i]))
        drain(started)
        total = squares_finish(it, 1, line_peers)
        count = 0.5 * jnp.sum(jnp.where(lane == 1, total, 0.0), axis=1, keepdims=True)
        total = jnp.sum(jnp.where(lane == 0, total, 0.0), axis=1, keepdims=True)
        rho = PENALTY * S * (total / count + 1e-06)
        gain = [
            0.5 * (gain[i] + (top + rho * target) / (den + rho))
            for i, (top, den, target) in enumerate(parts)
        ]
        if it + 1 < ITERS:
            for i in range(PAIRS):
                new_p[i] = turned(gain[i], i)
            spread(it + 1, new_p)
            crossed(2)
            for i, (p, den, turn) in enumerate(far):
                far_p[i] = 0.5 * (
                    p + (relay_buf[2, i] + den * p + rho * turn) / (den + rho)
                )
            for h in range(CHUNKS):
                relay(it + 1, far_p, h)
            spread_row(it + 1, new_p)
        started = len(pending)
        fit_start(it + 1, gain, dual)

    for i in range(PAIRS):
        solved[0, i] = gain[i]
    keep_gain = pltpu.make_async_copy(solved.at[0], solved_hbm.at[0], in_sem.at[7])
    keep_gain.start()
    drain(started)

    @pl.when(x != far_col)
    def _():
        for slot in range(GATHERS):
            for h in range(CHUNKS):
                to_far_col(slot, far_p, h).wait_send()

    smooth = fit_finish(ITERS)
    for i in range(PAIRS):
        value = dual[i] + gain[i] - smooth[i]
        solved[1, i] = value
    keep_dual = pltpu.make_async_copy(solved.at[1], solved_hbm.at[1], in_sem.at[8])
    keep_dual.start()

    drain(len(pending))
    keep_gain.wait()
    keep_dual.wait()


def placed(solved, gains_out, duals_out, dense, laid, in_sem, out_sem):
    loads = [
        pltpu.make_async_copy(solved.at[k], dense.at[k], in_sem.at[k]) for k in range(2)
    ]
    for load in loads:
        load.start()
    stores = []
    for k, out in enumerate((gains_out, duals_out)):
        loads[k].wait()
        for i in range(PAIRS):
            laid[k, 2 * i : 2 * i + 2] = dense[k, i].T.reshape(2, 4, 2, 8, OWNED)
        stores.append(pltpu.make_async_copy(laid.at[k], out, out_sem.at[k]))
        stores[k].start()
    for store in stores:
        store.wait()


def shards(vis, flags, positions, lmn, flux, gains, duals):
    hbm = pl.BlockSpec(memory_space=pltpu.HBM)
    positions = jnp.swapaxes(positions, 0, 1)
    dma = pltpu.SemaphoreType.DMA
    solved = pl.pallas_call(
        kernel,
        name="admm",
        out_shape=jax.ShapeDtypeStruct((2, PAIRS, OWNED, LANES), F32),
        in_specs=[pl.BlockSpec(memory_space=pltpu.HBM)] * 7,
        out_specs=hbm,
        scratch_shapes=[
            pltpu.VMEM(vis.shape, BF16),
            pltpu.VMEM(flags.shape, jnp.int32),
            pltpu.VMEM(positions.shape, F32),
            pltpu.VMEM(lmn.shape, F32),
            pltpu.VMEM(flux.shape, F32),
            pltpu.VMEM(gains.shape, F32),
            pltpu.VMEM(duals.shape, F32),
            pltpu.VMEM((8, 4, 64, 2 * LANES), F32),
            pltpu.VMEM((8, 4, 64, LANES), F32),
            pltpu.VMEM((8, 4, 2 * LANES, 2 * LANES), BF16),
            pltpu.VMEM((8, 64, 2 * LANES), BF16),
            pltpu.VMEM((8, 4, 64, 2 * LANES), F32),
            pltpu.VMEM((GATHERS, PAIRS, 64, LANES), F32),
            pltpu.VMEM((GATHERS, PAIRS, LANES, LANES), F32),
            pltpu.VMEM((CROSSED, PAIRS, OWNED, LANES), F32),
            pltpu.VMEM((CROSSED, PAIRS, OWNED, LANES), F32),
            pltpu.VMEM((ITERS, PAIRS, 64, LANES), F32),
            pltpu.VMEM((ITERS, 3, PAIRS, OWNED, LANES), F32),
            pltpu.VMEM((ITERS, PAIRS, LANES), F32),
            pltpu.VMEM((ITERS, 3, PAIRS, LANES), F32),
            pltpu.VMEM((ITERS + 1, 2, OWNED, LANES), F32),
            pltpu.VMEM((ITERS + 1, 7, 2, OWNED, LANES), F32),
            pltpu.VMEM((ITERS, 2, 1, LANES), F32),
            pltpu.VMEM((ITERS, 2, 15, 1, LANES), F32),
            pltpu.VMEM((PAIRS, LANES, LANES), F32),
            pltpu.VMEM((PAIRS, LANES, LANES), F32),
            pltpu.VMEM((LANES, LANES), F32),
            pltpu.VMEM((PAIRS, OWNED, LANES), F32),
            pltpu.VMEM((PAIRS, OWNED, LANES), F32),
            pltpu.VMEM((PAIRS, OWNED, LANES), F32),
            pltpu.VMEM((LANES, LANES), F32),
            pltpu.VMEM((PAIRS, LANES), F32),
            pltpu.VMEM((2, PAIRS, OWNED, LANES), F32),
            dma((9,)),
            dma((GATHERS, 3)), dma((GATHERS, 3)),
            dma((CROSSED, CHUNKS)), dma((CROSSED, CHUNKS)),
            dma((GATHERS, 4)), dma((GATHERS, 4, CHUNKS)),
            dma((GATHERS, 8, CHUNKS)),
            dma((ITERS, 3)), dma((ITERS, 3)),
            dma((ITERS, 3)), dma((ITERS, 3)),
            dma((ITERS, 2, 15)), dma((ITERS, 2, 15)),
            dma((ITERS + 1, 7)), dma((ITERS + 1, 7)),
        ],
        compiler_params=pltpu.CompilerParams(
            collective_id=0, has_side_effects=True, vmem_limit_bytes=60 * 1024 * 1024
        ),
    )(vis, flags, positions, lmn, flux, gains, duals)
    return pl.pallas_call(
        placed,
        name="placed",
        out_shape=(
            jax.ShapeDtypeStruct(gains.shape, F32),
            jax.ShapeDtypeStruct(duals.shape, F32),
        ),
        in_specs=[hbm],
        out_specs=(hbm, hbm),
        scratch_shapes=[
            pltpu.VMEM((2, PAIRS, OWNED, LANES), F32),
            pltpu.VMEM((2, *gains.shape), F32),
            dma((2,)), dma((2,)),
        ],
    )(solved)


def solution(mesh):
    finer = Mesh(mesh.devices.reshape(2, 4, mesh.shape["col"], 4, 2), AXES)
    return jax.shard_map(
        shards,
        mesh=finer,
        in_specs=(
            P(BAND, None, None, ROW, "x"),
            P(BAND, None, None),
            P(),
            P(),
            P(BAND, None),
            P(BAND, None, None, None, OWN),
            P(BAND, None, None, None, OWN),
        ),
        out_specs=(P(BAND, None, None, None, OWN), P(BAND, None, None, None, OWN)),
        check_vma=False,
    )
```
